512 devices in a mesh: dp: 8 (over x, y_hi), space: 64 (over y_lo, z, core).
Axes of the slice: x: 4, y: 4 (y_hi: 2, y_lo: 2; y = y_hi * 2 + y_lo), z: 16, core: 2. Of those that a mesh axis runs over, the one named last changes fastest.
Arguments:
- tiles_in: bfloat16 [8, 256, 8, 8, 384], P('dp', 'space'), may hold values from -6 to 6
- upstream: bfloat16 [8, 256, 8, 8, 384], P('dp', 'space'), may hold values from -1.1953125 to 1.1953125
- pool_weight: float32 [8, 256], P('dp', 'space'), may hold values from 0.25 to 4
- slide_cot: float32 [8, 384], P('dp'), may hold values from -6 to 6
- adjacency: int32 [8, 256, 8], P('dp', 'space'), may hold values from -1 to 255, as said below
- counts: int32 [8, 64], P('dp', 'space'), may hold values from 1 to 4, as said below
- kernel: float32 [7, 7, 384], replicated, may hold values from -0.875 to 0.875
- norm_gain: float32 [384], replicated, may hold values from 0.5 to 1.5
- w_in: bfloat16 [384, 1536], replicated, may hold values from -0.3125 to 0.3125
- w_out: bfloat16 [1536, 384], replicated, may hold values from -0.15625 to 0.15625
- layer_scale: float32 [384], replicated, may hold values from 0.1 to 1
Outputs:
- embedding: float32 [8, 384], P('dp')
- grad_tiles: bfloat16 [8, 256, 8, 8, 384], P('dp', 'space')
- grad_w_out: float32 [1536, 384], P('space')
- grad_kernel: float32 [7, 7, 384], replicated
The draws below stay inside these ranges and needn't reach their ends.
Inputs may be any that keep to these rules, and one draw needn't show every extreme that they name: Slots form blocks of 4; block k of a slide is one row of tiles, its live tiles in its first counts slots in column order; the last block of every slide is full, and often another one too. `adjacency`: tiles lie on a grid: entries 0, 4, 5 name live slots of the block before the tile's own, entries 1, 6, 7 of the block after it, entries 2 and 3 of its own block. The lists are mutual (b is the north neighbour of a exactly when a is the south neighbour of b, and likewise for the other directions). Slots that are not live have no neighbours and are named by none.
All inputs are finite; a program needn't handle non-finite values.
Results may differ from the reference program's by a relative error of at most 0.011.
Values may be sent and summed in bfloat16 or wider, within the bound.
A program may use at most 64 MiB of HBM per device.

```python
import math
import jax
import jax.numpy as jnp
from jax import lax

C = 384
HID = 1536
TILE = 8
CAP = 4
SLIDES = 8
SLOTS = 256


def geometry(key):
    blocks = SLOTS // CAP
    counts = jax.random.randint(jax.random.fold_in(key, 11), (SLIDES, blocks), 1, CAP + 1)
    fullest = jax.random.randint(jax.random.fold_in(key, 12), (SLIDES, 1), 0, blocks)
    block_ids = jnp.arange(blocks)[None, :]
    counts = jnp.where((block_ids == fullest) | (block_ids == blocks - 1), CAP, counts)
    offsets = jax.random.randint(jax.random.fold_in(key, 13), (SLIDES, blocks), 0, CAP + 1)
    return (counts.astype(jnp.int32), offsets.astype(jnp.int32))


def draw_counts(key, part):
    return geometry(key)[0]


def draw_adjacency(key, part):
    counts, offsets = geometry(key)
    blocks = SLOTS // CAP
    block_ids = jnp.arange(blocks, dtype=jnp.int32)
    slot_ids = jnp.arange(CAP, dtype=jnp.int32)
    column = offsets[:, :, None] + slot_ids[None, None, :]
    alive = slot_ids[None, None, :] < counts[:, :, None]
    moves = [(-1, 0), (1, 0), (0, -1), (0, 1), (-1, -1), (-1, 1), (1, -1), (1, 1)]
    lists = []
    for block_step, column_step in moves:
        other = block_ids + block_step
        inside = (other >= 0) & (other < blocks)
        clipped = jnp.clip(other, 0, blocks - 1)
        other_offset = offsets[:, clipped]
        other_count = counts[:, clipped]
        target = column + column_step - other_offset[:, :, None]
        usable = alive & inside[None, :, None] & (target >= 0) & (target < other_count[:, :, None])
        target_slot = clipped[None, :, None] * CAP + target
        lists.append(jnp.where(usable, target_slot, -1))
    return jnp.stack(lists, axis=-1).reshape(SLIDES, SLOTS, 8).astype(jnp.int32)


def levels(rng, dims, cuts, low, high):
    level = 1.0
    for position, blocks in cuts:
        draws = jax.random.uniform(jax.random.fold_in(jax.random.fold_in(rng, 6), position), (blocks,), jnp.float32, low / len(cuts), high / len(cuts))
        level = level * jnp.repeat(jnp.exp(draws), dims[position] // blocks).reshape((-1,) + (1,) * (len(dims) - 1 - position))
    return level


def normal_values(own_key, extent, spread, bound, split=(), held_as=jnp.bfloat16):
    gain = levels(own_key, extent, split, -0.22, 0.18) if split else 1.0
    array = jax.random.normal(own_key, extent, jnp.float32) * spread * gain
    return jnp.minimum(jnp.maximum(array, -bound), bound).astype(held_as)


def setup_inputs(seed: int = 0) -> dict:
    seeds = jax.random.split(jax.random.key(seed), 12)
    tiles_in = normal_values(seeds[0], (SLIDES, SLOTS, TILE, TILE, C), 1.0, 6.0, ((0, 8), (1, 64)))
    upstream = normal_values(seeds[1], (SLIDES, SLOTS, TILE, TILE, C), 0.2, 1.1953125, ((0, 8), (1, 64)))
    pool_weight = jnp.clip(jnp.exp(math.log(4.0) - 2.7725887 * jax.random.uniform(seeds[2], (SLIDES, SLOTS), jnp.float32) ** levels(seeds[2], (SLIDES, SLOTS), ((0, 8), (1, 64)), -0.2, 0.2)), 0.25, 4.0)
    slide_cot = normal_values(seeds[3], (SLIDES, C), 1.0, 6.0, ((0, 8),), jnp.float32)
    adjacency = draw_adjacency(jax.random.fold_in(seeds[11], 71), 0)
    counts = draw_counts(jax.random.fold_in(seeds[11], 71), 0)
    kernel = normal_values(seeds[6], (7, 7, C), 49 ** -0.5, 0.875, (), jnp.float32)
    norm_gain = jnp.clip(1.0 + 0.1 * jax.random.normal(seeds[7], (C,), jnp.float32), 0.5, 1.5)
    w_in = normal_values(seeds[8], (C, HID), C ** -0.5, 0.3125)
    w_out = normal_values(seeds[9], (HID, C), HID ** -0.5, 0.15625)
    layer_scale = jnp.clip(jnp.exp(jax.random.uniform(seeds[10], (C,), jnp.float32, math.log(0.1), math.log(1.0))), 0.1, 1.0)
    return dict(tiles_in=tiles_in, upstream=upstream, pool_weight=pool_weight, slide_cot=slide_cot, adjacency=adjacency, counts=counts, kernel=kernel, norm_gain=norm_gain, w_in=w_in, w_out=w_out, layer_scale=layer_scale)


sqrt_half = 0.7071067811865476
inv_root_two_pi = 0.3989422804014327

def depthwise(padded, kernel, tile_side):
    total = jnp.zeros(padded.shape[:1] + (tile_side, tile_side, padded.shape[3]), jnp.float32)
    for row_tap in range(7):
        for col_tap in range(7):
            window = padded[:, row_tap:row_tap + tile_side, col_tap:col_tap + tile_side, :].astype(jnp.float32)
            total = total + window * kernel[row_tap, col_tap]
    return total

def pick(source, wanted, offset):
    valid = wanted >= 0
    index = jnp.clip(wanted - offset, 0, source.shape[0] - 1).astype(jnp.int32)
    chosen = jnp.take(source, index, axis=0)
    return jnp.where(valid[:, None, None, None], chosen, jnp.zeros_like(chosen))

def frame(own, north_rows, south_rows, right_cols, left_cols, wanted, north_base, own_base, south_base):
    tile_side = own.shape[1]
    upper = jnp.concatenate([pick(north_rows, wanted[:, 4], north_base)[:, :, tile_side - 3:], pick(north_rows, wanted[:, 0], north_base), pick(north_rows, wanted[:, 5], north_base)[:, :, :3]], axis=2)
    middle = jnp.concatenate([pick(right_cols, wanted[:, 2], own_base), own, pick(left_cols, wanted[:, 3], own_base)], axis=2)
    lower = jnp.concatenate([pick(south_rows, wanted[:, 6], south_base)[:, :, tile_side - 3:], pick(south_rows, wanted[:, 1], south_base), pick(south_rows, wanted[:, 7], south_base)[:, :, :3]], axis=2)
    return jnp.concatenate([upper, middle, lower], axis=1)

def block_pass(padded, own, upstream, pool_weight, live, slide_cot, kernel, norm_gain, w_in, w_out, layer_scale):
    tile_side = own.shape[1]
    channels = own.shape[3]
    conv_out = depthwise(padded, kernel, tile_side)
    centred = conv_out - lax.optimization_barrier(jnp.mean(conv_out, axis=-1, keepdims=True))
    inv_std = lax.rsqrt(lax.optimization_barrier(jnp.mean(centred * centred, axis=-1, keepdims=True)) + 1e-06)
    normed = centred * inv_std
    lifted = (normed * norm_gain).astype(jnp.bfloat16).reshape(-1, channels)
    pre = jnp.dot(lifted, w_in, preferred_element_type=jnp.float32)
    cdf = 0.5 * (1.0 + jax.scipy.special.erf(pre * sqrt_half))
    activated = (pre * cdf).astype(jnp.bfloat16)
    mixed = jnp.dot(activated, w_out, preferred_element_type=jnp.float32).reshape(own.shape)
    block_out = own.astype(jnp.float32) + layer_scale * mixed
    weight_live = live * pool_weight
    emb_term = lax.optimization_barrier(jnp.sum(weight_live[:, None] * lax.optimization_barrier(jnp.sum(block_out, axis=(1, 2))), axis=0)) / tile_side
    extra = pool_weight[:, None] * slide_cot[None, :] / tile_side
    grad_out = live[:, None, None, None] * (upstream.astype(jnp.float32) + extra[:, None, None, :])
    grad_mixed = (grad_out * layer_scale).astype(jnp.bfloat16).reshape(-1, channels)
    grad_act = lax.dot_general(grad_mixed, w_out, (((1,), (1,)), ((), ())), preferred_element_type=jnp.float32)
    density = jnp.exp(-0.5 * pre * pre) * inv_root_two_pi
    grad_pre = (grad_act * (cdf + pre * density)).astype(jnp.bfloat16)
    grad_lift = lax.dot_general(grad_pre, w_in, (((1,), (1,)), ((), ())), preferred_element_type=jnp.float32)
    grad_normed = grad_lift.reshape(own.shape) * norm_gain
    grad_conv = inv_std * (grad_normed - lax.optimization_barrier(jnp.mean(grad_normed, axis=-1, keepdims=True)) - normed * lax.optimization_barrier(jnp.mean(grad_normed * normed, axis=-1, keepdims=True)))
    kernel_rows = []
    for row_tap in range(7):
        for col_tap in range(7):
            window = padded[:, row_tap:row_tap + tile_side, col_tap:col_tap + tile_side, :].astype(jnp.float32)
            kernel_rows.append(lax.optimization_barrier(jnp.sum(window * grad_conv, axis=(0, 1, 2))))
    kernel_grad = jnp.stack(kernel_rows).reshape(7, 7, channels)
    return (emb_term, grad_out, grad_conv, activated, grad_mixed, kernel_grad)

def reference(tiles_in, upstream, pool_weight, slide_cot, adjacency, counts, kernel, norm_gain, w_in, w_out, layer_scale):
    tile_side = TILE
    blocks = SLOTS // CAP
    embeddings = []
    gradients = []
    weight_total = jnp.zeros((HID, C), jnp.float32)
    kernel_total = jnp.zeros((7, 7, C), jnp.float32)
    for slide in range(SLIDES):
        own = tiles_in[slide]
        wanted = adjacency[slide]
        live = (jnp.arange(CAP, dtype=jnp.int32)[None, :] < counts[slide][:, None]).astype(jnp.float32).reshape(SLOTS)
        padded = frame(own, own[:, tile_side - 3:], own[:, :3], own[:, :, tile_side - 3:], own[:, :, :3], wanted, 0, 0, 0)
        cot = slide_cot[slide]

        def step(carry, parts):
            emb_acc, weight_acc, kernel_acc = carry
            pad_part, own_part, up_part, pool_part, live_part = parts
            emb_term, grad_out, grad_conv, activated, grad_mixed, kernel_grad = block_pass(pad_part, own_part, up_part, pool_part, live_part, cot, kernel, norm_gain, w_in, w_out, layer_scale)
            weight_acc = weight_acc + lax.dot_general(activated, grad_mixed, (((0,), (0,)), ((), ())), preferred_element_type=jnp.float32)
            return ((emb_acc + emb_term, weight_acc, kernel_acc + kernel_grad), (grad_out, grad_conv))
        parts = (padded.reshape((blocks, CAP) + padded.shape[1:]), own.reshape((blocks, CAP) + own.shape[1:]), upstream[slide].reshape((blocks, CAP) + own.shape[1:]), pool_weight[slide].reshape(blocks, CAP), live.reshape(blocks, CAP))
        start = (jnp.zeros((C,), jnp.float32), weight_total, kernel_total)
        (emb_sum, weight_total, kernel_total), (grad_out, grad_conv) = lax.scan(step, start, parts)
        grad_out = grad_out.reshape(own.shape)
        grad_conv = grad_conv.reshape(own.shape)
        padded_grad = frame(grad_conv, grad_conv[:, tile_side - 3:], grad_conv[:, :3], grad_conv[:, :, tile_side - 3:], grad_conv[:, :, :3], wanted, 0, 0, 0)
        back = depthwise(padded_grad, kernel[::-1, ::-1], tile_side)
        gradients.append(((grad_out + back) * live[:, None, None, None]).astype(jnp.bfloat16))
        embeddings.append(emb_sum)
    return (jnp.stack(embeddings), jnp.stack(gradients), weight_total, kernel_total)
```

```python
import functools

import jax
import jax.numpy as jnp
from jax import lax
from jax.experimental import pallas as pl
from jax.experimental.pallas import tpu as pltpu
from jax.sharding import PartitionSpec as P

MESH = pl.DeviceIdType.MESH
F32, BF16 = jnp.float32, jnp.bfloat16
sqrt_half = 0.7071067811865476
inv_root_two_pi = 0.3989422804014327

C, HID, CAP, TILE = 384, 1536, 4, 8
CG = C // 128
PIX = CAP * TILE * TILE
CHUNK = 384
ROWS = 52


def spread(adj, t, pad, own, north, south):
    def entry(e):
        wanted = adj[t, e]
        return jnp.bitwise_and(jnp.maximum(wanted, 0), CAP - 1), wanted >= 0

    parts = (
        (3, 8, (own, 2), (own, None), (own, 3)),
        (0, 3, (north, 4), (north, 0), (north, 5)),
        (11, 3, (south, 6), (south, 1), (south, 7)),
    )
    for row, rows, *columns in parts:
        for place, (source, e) in enumerate(columns):
            if e is None:
                groups = source(t)
            else:
                index, valid = entry(e)
                groups = [jnp.where(valid, g, 0.0) for g in source(index)]
            for g in range(CG):
                pad[g, t, row : row + rows, 8 * place : 8 * place + 8, :] = groups[g]


def conv_tile(pad, taps, g, t, flip):
    total = [None] * TILE
    for j in range(7):
        column = [taps[g, 48 - (i * 7 + j) if flip else i * 7 + j] for i in range(7)]
        for r in range(14):
            window = pad[g, t, r, 5 + j : 13 + j, :]
            for i in range(7):
                a = r - i
                if 0 <= a < TILE:
                    term = window * column[i]
                    total[a] = term if total[a] is None else total[a] + term
    return total


def split_groups(value):
    return [value[..., g * 128 : (g + 1) * 128] for g in range(CG)]


def live_of(cnt, t):
    return jnp.where(t < cnt[0, 0], 1.0, 0.0).astype(F32)


def grad_out_of(up, pw, cot, live, t):
    extra = pw[0, t] * cot[...] / TILE
    return live * (up[t].astype(F32) + extra[None])


def load_taps(ker, taps):
    for ij in range(49):
        row = ker[ij // 7, ij % 7 : ij % 7 + 1, :]
        for g in range(CG):
            taps[g, ij] = jnp.broadcast_to(row[:, g * 128 : (g + 1) * 128], (8, 128))


def forward_backward(
    pw, adj, cnt, own, north, south, up, cot, ker, gain, scale, w_in_hbm, w_out_hbm,
    grads, emb, gconv, edge_first, edge_last,
    pad, taps, normed, inv, lifted, gmix, glift, w_in, w_out, sems,
):
    loads = [
        pltpu.make_async_copy(w_in_hbm, w_in, sems.at[0]),
        pltpu.make_async_copy(w_out_hbm, w_out, sems.at[1]),
    ]
    for load in loads:
        load.start()
    load_taps(ker, taps)

    def groups_of(ref):
        return lambda i: split_groups(ref[i].astype(F32))

    @pl.loop(0, CAP)
    def _(t):
        spread(adj, t, pad, groups_of(own), groups_of(north), groups_of(south))

    @pl.loop(0, CAP)
    def _(t):
        @pl.loop(0, CG)
        def _(g):
            rows = conv_tile(pad, taps, g, t, False)
            for a in range(TILE):
                normed[g, t, a] = rows[a]

    emb_own = jnp.zeros((1, C), F32)
    for t in range(CAP):
        live = live_of(cnt, t)
        x = [normed[g, t].reshape(64, 128) for g in range(CG)]
        mean = jnp.sum(x[0] + x[1] + x[2], axis=-1, keepdims=True) / C
        x = [v - mean for v in x]
        var = jnp.sum(x[0] * x[0] + x[1] * x[1] + x[2] * x[2], axis=-1, keepdims=True) / C
        istd = jnp.broadcast_to(lax.rsqrt(var + 1e-06), (64, 128))
        inv[t] = istd
        here = slice(t * 64, t * 64 + 64)
        for g in range(CG):
            lanes = slice(g * 128, g * 128 + 128)
            n = x[g] * istd
            normed[g, t] = n.reshape(TILE, TILE, 128)
            lifted[here, lanes] = (n * gain[:, lanes]).astype(BF16)
        g_out = grad_out_of(up, pw, cot, live, t)
        gmix[here, :] = (g_out * scale[...][None]).astype(BF16).reshape(64, C)
        weight = live * pw[0, t]
        emb_own = emb_own + weight * jnp.sum(own[t].astype(F32).reshape(64, C), axis=0, keepdims=True)

    for load in loads:
        load.wait()
    mixed = jnp.zeros((8, C), F32)
    for h in range(HID // CHUNK):
        here = slice(h * CHUNK, (h + 1) * CHUNK)
        pre = jnp.dot(lifted[...], w_in[:, here], preferred_element_type=F32)
        cdf = 0.5 * (1.0 + lax.erf(pre * sqrt_half))
        act = (pre * cdf).astype(BF16)
        gact = lax.dot_general(
            gmix[...], w_out[here, :], (((1,), (1,)), ((), ())), preferred_element_type=F32
        )
        density = jnp.exp(-0.5 * pre * pre) * inv_root_two_pi
        gpre = (gact * (cdf + pre * density)).astype(BF16)
        gl = lax.dot_general(
            gpre, w_in[:, here], (((1,), (1,)), ((), ())), preferred_element_type=F32
        )
        if h == 0:
            glift[...] = gl
        else:
            glift[...] += gl
        pooled = jnp.zeros((1, CHUNK), F32)
        for t in range(CAP):
            weight = live_of(cnt, t) * pw[0, t]
            pooled = pooled + weight * jnp.sum(
                act[t * 64 : t * 64 + 64].astype(F32), axis=0, keepdims=True
            )
        high = pooled.astype(BF16)
        rest = pooled - high.astype(F32)
        middle = rest.astype(BF16)
        low = (rest - middle.astype(F32)).astype(BF16)
        three = jnp.concatenate([high, middle, low, jnp.zeros((5, CHUNK), BF16)], axis=0)
        mixed = mixed + jnp.dot(three, w_out[here, :], preferred_element_type=F32)
        gw = lax.dot_general(
            act, gmix[...], (((0,), (0,)), ((), ())), preferred_element_type=F32
        ).astype(BF16)
        for q in range(CHUNK // 24):
            block = h * (CHUNK // 24) + q
            core, plane, z = block % 2, block // 32, block // 2 % 16
            chunk, row = z // 2 * 2 + plane, z % 2 * 24
            grads[core, chunk, row : row + 24, :] = gw[q * 24 : q * 24 + 24, :]
    mix = jnp.sum(mixed, axis=0, keepdims=True)
    emb[...] = jnp.broadcast_to((emb_own + scale[...] * mix) / TILE, (8, C))

    for t in range(CAP):
        here = slice(t * 64, t * 64 + 64)
        gn = [glift[here, g * 128 : g * 128 + 128] * gain[:, g * 128 : g * 128 + 128] for g in range(CG)]
        n = [normed[g, t].reshape(64, 128) for g in range(CG)]
        m1 = jnp.sum(gn[0] + gn[1] + gn[2], axis=-1, keepdims=True) / C
        m2 = jnp.sum(gn[0] * n[0] + gn[1] * n[1] + gn[2] * n[2], axis=-1, keepdims=True) / C
        for g in range(CG):
            gc = (inv[t] * (gn[g] - m1 - n[g] * m2)).reshape(TILE, TILE, 128)
            gconv[g, t] = gc
            edge_first[g, t] = gc[:3].astype(BF16)
            edge_last[g, t] = gc[TILE - 3 :].astype(BF16)

    for g in range(CG):
        lanes = slice(g * 128, g * 128 + 128)
        for j in range(7):

            def tile_taps(t, carry, j=j, g=g):
                gc = [gconv[g, t, a] for a in range(TILE)]
                out = list(carry)
                for r in range(14):
                    window = pad[g, t, r, 5 + j : 13 + j, :]
                    for i in range(7):
                        a = r - i
                        if 0 <= a < TILE:
                            out[i] = out[i] + window * gc[a]
                return tuple(out)

            sums = lax.fori_loop(
                0, CAP, tile_taps, tuple(jnp.zeros((8, 128), F32) for _ in range(7))
            )
            for i in range(7):
                taps[g, i * 7 + j] = sums[i]
        total = jnp.sum(taps[g], axis=1)
        total = jnp.concatenate([total, jnp.zeros((15, 128), F32)], axis=0)
        for chunk in range(16):
            part = total[chunk * 4 : chunk * 4 + 4].astype(BF16)
            for core in range(2):
                grads[core, chunk, 48:52, lanes] = part


def reduce_kernel(
    spaces, first, last, grads, emb,
    north_out, south_out, w_out, k_out, emb_out,
    got1, emb1, send2, got2, emb_sum, emb2, send3, got3, send4w, send4k, half, other,
    s_halo, r_halo, s1, r1, s2, r2, s_e, r_e, s3, r3, s4w, r4w, s4k, r4k, s5, r5,
):
    dp, space = lax.axis_index("dp"), lax.axis_index("space")
    core = lax.rem(space, 2)
    z = lax.rem(space // 2, 16)
    plane = space // 32
    spot = dp * 2 + plane

    def at(d, p, zz, c):
        return (d, (p * 16 + zz) * 2 + c)

    def chunk_device(q):
        return at(q // 2, lax.rem(q, 2), z, core)

    partner = at(dp, plane, z, 1 - core)
    before = (dp, lax.rem(space + spaces - 1, spaces))
    after = (dp, lax.rem(space + 1, spaces))
    home_z = 2 * dp + z // 8

    barrier = pltpu.get_barrier_semaphore()

    def greet(device):
        pl.semaphore_signal(barrier, inc=1, device_id=device, device_id_type=MESH)

    greet(partner)
    greet(before)
    greet(after)

    @pl.loop(1, 16)
    def _(k):
        greet(chunk_device(lax.rem(spot + k, 16)))
        greet(at(dp, plane, lax.rem(z + k, 16), core))

    own_home = home_z == z

    @pl.loop(0, 8)
    def _(k):
        mine = jnp.logical_and(own_home, k == lax.rem(z, 8))

        @pl.when(jnp.logical_not(mine))
        def _():
            greet(at(z // 2, plane, 8 * lax.rem(z, 2) + k, core))

    @pl.when(own_home)
    def _():
        pl.semaphore_wait(barrier, 3 + 30 + 7)

    @pl.when(jnp.logical_not(own_home))
    def _():
        pl.semaphore_wait(barrier, 3 + 30 + 8)

    def copy(src, dst, send, recv, device):
        return pltpu.make_async_remote_copy(
            src_ref=src, dst_ref=dst, send_sem=send, recv_sem=recv,
            device_id=device, device_id_type=MESH,
        )

    pair = copy(grads.at[1 - core], got1, s1.at[0], r1.at[0], partner)
    pair_emb = copy(emb, emb1, s1.at[1], r1.at[1], partner)
    pair.start()
    pair_emb.start()
    to_after = copy(last, north_out, s_halo.at[0], r_halo.at[0], after)
    to_before = copy(first, south_out, s_halo.at[1], r_halo.at[1], before)
    to_after.start()
    to_before.start()
    pair_emb.wait()
    emb_sum[...] = emb[...] + emb1[...]
    across = copy(emb_sum, emb2, s_e.at[0], r_e.at[0], at(dp, 1 - plane, z, core))
    across.start()
    pair.wait()

    def sum2(q):
        send2[q] = (grads[core, q].astype(F32) + got1[q].astype(F32)).astype(BF16)

    @pl.loop(1, 16)
    def _(k):
        q = lax.rem(spot + k, 16)
        sum2(q)
        copy(send2.at[q], got2.at[spot], s2.at[k], r2.at[spot], chunk_device(q)).start()

    sum2(spot)
    got2[spot] = send2[spot]
    across.wait()
    emb_both = emb_sum[0:1] + emb2[0:1]
    high = emb_both.astype(BF16)
    low = emb_both - high.astype(F32)
    mine = jnp.where(core == 0, high.astype(F32), low)

    @pl.loop(1, 16)
    def _(k):
        q = lax.rem(spot + k, 16)
        copy(send2.at[q], got2.at[q], s2.at[k], r2.at[q], chunk_device(q)).wait()

    total = got2[0].astype(F32)
    for q in range(1, 16):
        total = total + got2[q].astype(F32)

    tail = total[48:52]
    for q in range(16):
        send3[q] = jnp.concatenate([total[q * 3 : q * 3 + 3], tail, mine], axis=0).astype(BF16)

    @pl.loop(1, 16)
    def _(k):
        q = lax.rem(z + k, 16)
        copy(send3.at[q], got3.at[z], s3.at[k], r3.at[z], at(dp, plane, q, core)).start()

    got3[z] = send3[z]

    @pl.loop(1, 16)
    def _(k):
        q = lax.rem(z + k, 16)
        copy(send3.at[q], got3.at[q], s3.at[k], r3.at[q], at(dp, plane, q, core)).wait()

    total = got3[0].astype(F32)
    for q in range(1, 16):
        total = total + got3[q].astype(F32)

    send4w[...] = total[0:3].astype(BF16)
    send4k[...] = total[3:7].astype(BF16)
    half[...] = jnp.broadcast_to(total[7:8], (8, C))
    swap = copy(half, other, s5.at[0], r5.at[0], partner)
    swap.start()

    @pl.loop(0, 8)
    def _(d):
        mine = jnp.logical_and(own_home, d == dp)

        @pl.when(jnp.logical_not(mine))
        def _():
            copy(
                send4w, w_out.at[lax.rem(z, 8)], s4w.at[d], r4w.at[lax.rem(z, 8)],
                at(d, plane, home_z, core),
            ).start()

        @pl.when(mine)
        def _():
            w_out[lax.rem(z, 8)] = send4w[...]

    @pl.loop(1, 16)
    def _(k):
        q = lax.rem(spot + k, 16)
        copy(send4k, k_out.at[spot], s4k.at[k], r4k.at[spot], chunk_device(q)).start()

    k_out[spot] = send4k[...]
    swap.wait()
    emb_out[...] = half[...] + other[...]

    @pl.loop(0, 8)
    def _(k):
        mine = jnp.logical_and(own_home, k == lax.rem(z, 8))
        sent = jnp.logical_and(own_home, k == dp)

        @pl.when(jnp.logical_not(mine))
        def _():
            copy(send4w, w_out.at[k], s4w.at[k], r4w.at[k], partner).wait_recv()

        @pl.when(jnp.logical_not(sent))
        def _():
            copy(send4w, w_out.at[k], s4w.at[k], r4w.at[k], partner).wait_send()

    @pl.loop(1, 16)
    def _(k):
        q = lax.rem(spot + k, 16)
        copy(send4k, k_out.at[q], s4k.at[k], r4k.at[q], chunk_device(q)).wait()

    to_after.wait()
    to_before.wait()


def back_kernel(
    pw, adj, cnt, up, cot, ker, gconv, north, south, w_got, k_got, emb_got,
    emb, out, w_grad, k_grad,
    pad, taps,
):
    load_taps(ker, taps)

    def from_tiles(i):
        return [gconv[g, i] for g in range(CG)]

    def from_edge(ref):
        return lambda i: [ref[g, i].astype(F32) for g in range(CG)]

    @pl.loop(0, CAP)
    def _(t):
        spread(adj, t, pad, from_tiles, from_edge(north), from_edge(south))

    @pl.loop(0, CAP)
    def _(t):
        live = live_of(cnt, t)
        for g in range(CG):
            lanes = slice(g * 128, g * 128 + 128)
            rows = conv_tile(pad, taps, g, t, True)
            extra = pw[0, t] * cot[:, lanes] / TILE
            for a in range(TILE):
                g_out = live * (up[t, a, :, lanes].astype(F32) + extra)
                out[t, a, :, lanes] = (live * (g_out + rows[a])).astype(BF16)

    emb[...] = emb_got[0:1]
    for k in range(8):
        w_grad[k * 3 : k * 3 + 3, :] = w_got[k].astype(F32)
    for ij in range(49):
        k_grad[ij // 7, ij % 7 : ij % 7 + 1, :] = k_got[ij // 4, ij % 4 : ij % 4 + 1, :].astype(F32)


VMEM = pl.BlockSpec(memory_space=pltpu.VMEM)
SMEM = pl.BlockSpec(memory_space=pltpu.SMEM)
HBM = pl.BlockSpec(memory_space=pl.ANY)


def vmem(shape, dtype):
    return pltpu.VMEM(shape, dtype)


def passed_along(value, axis, steps):
    count = lax.axis_size(axis)
    leading, last = (max(0, -steps), min(count, count - steps))
    return lax.ppermute(value, axis, [(source, source + steps) for source in range(leading, last)])


def per_device(
    tiles_in, upstream, pool_weight, slide_cot, adjacency, counts, kernel, norm_gain, w_in, w_out,
    layer_scale,
):
    own, up = tiles_in[0], upstream[0]
    adj = adjacency[0]
    north = passed_along(own[:, TILE - 3 :], "space", 1)
    south = passed_along(own[:, :3], "space", -1)
    spaces = lax.axis_size("space")
    struct = jax.ShapeDtypeStruct
    pad = vmem((CG, CAP, 14, 24, 128), F32)
    taps = vmem((CG, 49, 8, 128), F32)
    edge = (CG, CAP, 3, TILE, 128)

    grads, emb, gconv, first, last = pl.pallas_call(
        forward_backward,
        out_shape=(
            struct((2, 16, ROWS, C), BF16),
            struct((8, C), F32),
            struct((CG, CAP, TILE, TILE, 128), F32),
            struct(edge, BF16),
            struct(edge, BF16),
        ),
        in_specs=[SMEM] * 3 + [VMEM] * 8 + [HBM] * 2,
        out_specs=(VMEM,) * 5,
        scratch_shapes=[
            pad,
            taps,
            vmem((CG, CAP, TILE, TILE, 128), F32),
            vmem((CAP, 64, 128), F32),
            vmem((PIX, C), BF16),
            vmem((PIX, C), BF16),
            vmem((PIX, C), F32),
            vmem((C, HID), BF16),
            vmem((HID, C), BF16),
            pltpu.SemaphoreType.DMA((2,)),
        ],
        compiler_params=pltpu.CompilerParams(vmem_limit_bytes=40 << 20),
        name="forward_backward",
    )(
        pool_weight, adj, counts, own, north, south, up, slide_cot, kernel, norm_gain[None],
        layer_scale[None], w_in, w_out,
    )

    dma = pltpu.SemaphoreType.DMA
    north_g, south_g, w_got, k_got, emb_got = pl.pallas_call(
        functools.partial(reduce_kernel, spaces),
        out_shape=(
            struct(edge, BF16),
            struct(edge, BF16),
            struct((8, 3, C), BF16),
            struct((16, 4, C), BF16),
            struct((8, C), F32),
        ),
        in_specs=[VMEM] * 4,
        out_specs=(VMEM,) * 5,
        scratch_shapes=[
            vmem((16, ROWS, C), BF16),
            vmem((8, C), F32),
            vmem((16, ROWS, C), BF16),
            vmem((16, ROWS, C), BF16),
            vmem((8, C), F32),
            vmem((8, C), F32),
            vmem((16, 8, C), BF16),
            vmem((16, 8, C), BF16),
            vmem((3, C), BF16),
            vmem((4, C), BF16),
            vmem((8, C), F32),
            vmem((8, C), F32),
            dma((2,)), dma((2,)),
            dma((2,)), dma((2,)),
            dma((16,)), dma((16,)),
            dma((1,)), dma((1,)),
            dma((16,)), dma((16,)),
            dma((8,)), dma((8,)),
            dma((16,)), dma((16,)),
            dma((1,)), dma((1,)),
        ],
        compiler_params=pltpu.CompilerParams(
            collective_id=0, has_side_effects=True, vmem_limit_bytes=40 << 20
        ),
        name="reduce_gradients",
    )(first, last, grads, emb)

    embedding, grad_tiles, w_grad, k_grad = pl.pallas_call(
        back_kernel,
        out_shape=(
            struct((1, C), F32),
            struct((CAP, TILE, TILE, C), BF16),
            struct((24, C), F32),
            struct((7, 7, C), F32),
        ),
        in_specs=[SMEM] * 3 + [VMEM] * 9,
        out_specs=(VMEM,) * 4,
        scratch_shapes=[pad, taps],
        compiler_params=pltpu.CompilerParams(vmem_limit_bytes=40 << 20),
        name="back",
    )(
        pool_weight, adj, counts, up, slide_cot, kernel, gconv, north_g, south_g, w_got, k_got,
        emb_got,
    )
    return embedding, grad_tiles[None], w_grad, k_grad


def solution(mesh):
    return jax.shard_map(
        per_device,
        mesh=mesh,
        in_specs=(
            P("dp", "space", None, None, None),
            P("dp", "space", None, None, None),
            P("dp", "space"),
            P("dp", None),
            P("dp", "space", None),
            P("dp", "space"),
            P(),
            P(),
            P(),
            P(),
            P(),
        ),
        out_specs=(P("dp", None), P("dp", "space", None, None, None), P("space", None), P()),
        check_vma=False,
    )
```

```python
import functools

import jax
import jax.numpy as jnp
from jax import lax
from jax.experimental import pallas as pl
from jax.experimental.pallas import tpu as pltpu
from jax.sharding import PartitionSpec as P

MESH = pl.DeviceIdType.MESH
F32, BF16 = jnp.float32, jnp.bfloat16
sqrt_half = 0.7071067811865476
inv_root_two_pi = 0.3989422804014327

C, HID, CAP, TILE = 384, 1536, 4, 8
CG = C // 128
PIX = CAP * TILE * TILE
CHUNK = 384


def spread(adj, t, pad, own, north, south):
    def entry(e):
        wanted = adj[t, e]
        return jnp.bitwise_and(jnp.maximum(wanted, 0), CAP - 1), wanted >= 0

    parts = (
        (3, 8, (own, 2), (own, None), (own, 3)),
        (0, 3, (north, 4), (north, 0), (north, 5)),
        (11, 3, (south, 6), (south, 1), (south, 7)),
    )
    for row, rows, *columns in parts:
        for place, (source, e) in enumerate(columns):
            if e is None:
                groups = source(t)
            else:
                index, valid = entry(e)
                groups = [jnp.where(valid, g, 0.0) for g in source(index)]
            for g in range(CG):
                pad[g, t, row : row + rows, 8 * place : 8 * place + 8, :] = groups[g]


def conv_tile(pad, taps, g, t, flip):
    total = [None] * TILE
    for j in range(7):
        column = [taps[g, 48 - (i * 7 + j) if flip else i * 7 + j] for i in range(7)]
        for r in range(14):
            window = pad[g, t, r, 5 + j : 13 + j, :]
            for i in range(7):
                a = r - i
                if 0 <= a < TILE:
                    term = window * column[i]
                    total[a] = term if total[a] is None else total[a] + term
    return total


def split_groups(value):
    return [value[..., g * 128 : (g + 1) * 128] for g in range(CG)]


def live_of(cnt, t):
    return jnp.where(t < cnt[0, 0], 1.0, 0.0).astype(F32)


def grad_out_of(up, pw, cot, live, t):
    extra = pw[0, t] * cot[...] / TILE
    return live * (up[t].astype(F32) + extra[None])


def load_taps(ker, taps):
    for ij in range(49):
        row = ker[ij // 7, ij % 7 : ij % 7 + 1, :]
        for g in range(CG):
            taps[g, ij] = jnp.broadcast_to(row[:, g * 128 : (g + 1) * 128], (8, 128))


def copy_to(device, src, dst, send, recv):
    return pltpu.make_async_remote_copy(
        src_ref=src, dst_ref=dst, send_sem=send, recv_sem=recv,
        device_id=device, device_id_type=MESH,
    )


def greet(device):
    pl.semaphore_signal(
        pltpu.get_barrier_semaphore(), inc=1, device_id=device, device_id_type=MESH
    )


def halo_kernel(spaces, own, north, south, send, recv):
    dp, space = lax.axis_index("dp"), lax.axis_index("space")
    before = (dp, lax.rem(space + spaces - 1, spaces))
    after = (dp, lax.rem(space + 1, spaces))
    greet(before)
    greet(after)
    pl.semaphore_wait(pltpu.get_barrier_semaphore(), 2)
    down = copy_to(after, own.at[:, TILE - 3 :], north, send.at[0], recv.at[0])
    up = copy_to(before, own.at[:, :3], south, send.at[1], recv.at[1])
    down.start()
    up.start()
    down.wait()
    up.wait()


def main_kernel(
    spaces,
    pw, adj, cnt,
    own_in, north_in, south_in, up_in, cot_in, ker_in, gain_in, scale_in, w_in_in, w_out_in,
    out, got4, emb_out,
    own, north, south, up, cot, ker, gain, scale, w_in, w_out, load_sems,
    pad, pad_g, taps, normed, inv, lifted, gmix, glift, slope, gconv, kparts,
    grads, got1, send2, got2, kgrads, kgot1, ksend2, kgot2,
    emb, emb1, emb_sum, emb2, send3, got3, send4, half, other,
    edge_first, edge_last, north_g, south_g,
    s_halo, r_halo, s1, r1, s1k, r1k, s2, r2, s2k, r2k, s_e, r_e, s3, r3, s4, r4, s5, r5,
):
    dp, space = lax.axis_index("dp"), lax.axis_index("space")
    core = lax.rem(space, 2)
    z = lax.rem(space // 2, 16)
    plane = space // 32
    spot = dp * 2 + plane

    def at(d, p, zz):
        return (d, (p * 16 + zz) * 2 + core)

    def chunk_device(q):
        return at(q // 2, lax.rem(q, 2), z)

    partner = (dp, space + 1 - 2 * core)
    before = (dp, lax.rem(space + spaces - 1, spaces))
    after = (dp, lax.rem(space + 1, spaces))

    loads = {}
    sources = (
        (own_in, own), (north_in, north), (south_in, south), (ker_in, ker), (gain_in, gain),
        (up_in, up), (cot_in, cot), (scale_in, scale), (w_in_in, w_in), (w_out_in, w_out),
    )
    for n, (src, dst) in enumerate(sources):
        loads[n] = pltpu.make_async_copy(src, dst, load_sems.at[n])
        loads[n].start()

    greet(partner)
    greet(before)
    greet(after)

    @pl.loop(1, 16)
    def _(k):
        greet(at(dp, plane, lax.rem(z + k, 16)))
        greet(chunk_device(lax.rem(spot + k, 16)))

    loads[3].wait()
    load_taps(ker, taps)
    for n in (0, 1, 2):
        loads[n].wait()

    def groups_of(ref):
        return lambda i: split_groups(ref[i].astype(F32))

    @pl.loop(0, CAP)
    def _(t):
        spread(adj, t, pad, groups_of(own), groups_of(north), groups_of(south))

    @pl.loop(0, CAP)
    def _(t):
        @pl.loop(0, CG)
        def _(g):
            rows = conv_tile(pad, taps, g, t, False)
            for a in range(TILE):
                normed[g, t, a] = rows[a]

    for n in (4, 5, 6, 7):
        loads[n].wait()
    emb_own = jnp.zeros((1, C), F32)
    for t in range(CAP):
        live = live_of(cnt, t)
        x = [normed[g, t].reshape(64, 128) for g in range(CG)]
        mean = jnp.sum(x[0] + x[1] + x[2], axis=-1, keepdims=True) / C
        x = [v - mean for v in x]
        var = jnp.sum(x[0] * x[0] + x[1] * x[1] + x[2] * x[2], axis=-1, keepdims=True) / C
        istd = jnp.broadcast_to(lax.rsqrt(var + 1e-06), (64, 128))
        inv[t] = istd
        here = slice(t * 64, t * 64 + 64)
        for g in range(CG):
            lanes = slice(g * 128, g * 128 + 128)
            n = x[g] * istd
            normed[g, t] = n.reshape(TILE, TILE, 128)
            lifted[here, lanes] = (n * gain[:, lanes]).astype(BF16)
        g_out = grad_out_of(up, pw, cot, live, t)
        gmix[here, :] = (g_out * scale[...][None]).astype(BF16).reshape(64, C)
        weight = live * pw[0, t]
        emb_own = emb_own + weight * jnp.sum(own[t].astype(F32).reshape(64, C), axis=0, keepdims=True)

    d = lax.broadcasted_iota(jnp.int32, (8, CHUNK), 1)
    d_core = jnp.where(d >= 192, 1, 0)
    d = d - 192 * d_core
    d_dp = jnp.zeros_like(d)
    for m in range(1, 8):
        d_dp = d_dp + jnp.where(d >= 24 * m, 1, 0)
    d = d - 24 * d_dp
    d_z = jnp.zeros_like(d)
    for m in range(1, 8):
        d_z = d_z + jnp.where(d >= 3 * m, 1, 0)
    d = d - 3 * d_z
    source = d_z * 48 + d_core * 24 + d_dp * 3 + d
    rows = lax.broadcasted_iota(jnp.int32, (CHUNK, CHUNK), 0)
    order = jnp.where(rows == source[0:1], 1.0, 0.0).astype(BF16)

    loads[8].wait()
    loads[9].wait()

    def pair_of(h):
        return copy_to(partner, grads.at[1 - core, h], got1.at[h], s1.at[h], r1.at[h])

    def plane_of(h, k):
        to = lax.rem(dp + k, 8)
        return copy_to(
            at(to, h // 2, z), send2.at[h, to], got2.at[spot, h % 2], s2.at[h, k],
            r2.at[spot, h % 2],
        )

    def pass_on(h):
        pair_of(h).wait_recv()
        send2[h] = (grads[core, h].astype(F32) + got1[h].astype(F32)).astype(BF16)

        @pl.loop(1, 8)
        def _(k):
            plane_of(h, k).start()

        @pl.when(plane == h // 2)
        def _():
            got2[spot, h % 2] = send2[h, dp]

        @pl.when(plane != h // 2)
        def _():
            plane_of(h, 0).start()

    mixed = jnp.zeros((8, C), F32)
    for h in range(HID // CHUNK):
        here = slice(h * CHUNK, (h + 1) * CHUNK)
        pre = jnp.dot(lifted[...], w_in[:, here], preferred_element_type=F32)
        cdf = 0.5 * (1.0 + lax.erf(pre * sqrt_half))
        act = (pre * cdf).astype(BF16)
        density = jnp.exp(-0.5 * pre * pre) * inv_root_two_pi
        slope[:, here] = cdf + pre * density
        sent = jnp.dot(act, order, preferred_element_type=F32).astype(BF16)
        gw = lax.dot_general(
            sent, gmix[...], (((0,), (0,)), ((), ())), preferred_element_type=F32
        ).astype(BF16)
        for c in range(2):
            for m in range(8):
                grads[c, h, m] = gw[(c * 8 + m) * 24 : (c * 8 + m) * 24 + 24]
        if h == 0:
            pl.semaphore_wait(pltpu.get_barrier_semaphore(), 33)
        pair_of(h).start()
        pooled = jnp.zeros((1, CHUNK), F32)
        for t in range(CAP):
            weight = live_of(cnt, t) * pw[0, t]
            pooled = pooled + weight * jnp.sum(
                act[t * 64 : t * 64 + 64].astype(F32), axis=0, keepdims=True
            )
        high = pooled.astype(BF16)
        rest = pooled - high.astype(F32)
        middle = rest.astype(BF16)
        low = (rest - middle.astype(F32)).astype(BF16)
        three = jnp.concatenate([high, middle, low, jnp.zeros((5, CHUNK), BF16)], axis=0)
        mixed = mixed + jnp.dot(three, w_out[here, :], preferred_element_type=F32)
        if h > 0:
            pass_on(h - 1)
    mix = jnp.sum(mixed, axis=0, keepdims=True)
    emb[...] = jnp.broadcast_to((emb_own + scale[...] * mix) / TILE, (8, C))
    emb_pair = copy_to(partner, emb, emb1, s_e.at[0], r_e.at[0])
    emb_pair.start()

    for h in range(HID // CHUNK):
        here = slice(h * CHUNK, (h + 1) * CHUNK)
        gact = lax.dot_general(
            gmix[...], w_out[here, :], (((1,), (1,)), ((), ())), preferred_element_type=F32
        )
        gpre = (gact * slope[:, here]).astype(BF16)
        gl = lax.dot_general(
            gpre, w_in[:, here], (((1,), (1,)), ((), ())), preferred_element_type=F32
        )
        if h == 0:
            glift[...] = gl
            pass_on(HID // CHUNK - 1)
        else:
            glift[...] += gl

    for t in range(CAP):
        here = slice(t * 64, t * 64 + 64)
        gn = [glift[here, g * 128 : g * 128 + 128] * gain[:, g * 128 : g * 128 + 128] for g in range(CG)]
        n = [normed[g, t].reshape(64, 128) for g in range(CG)]
        m1 = jnp.sum(gn[0] + gn[1] + gn[2], axis=-1, keepdims=True) / C
        m2 = jnp.sum(gn[0] * n[0] + gn[1] * n[1] + gn[2] * n[2], axis=-1, keepdims=True) / C
        for g in range(CG):
            gc = (inv[t] * (gn[g] - m1 - n[g] * m2)).reshape(TILE, TILE, 128)
            gconv[g, t] = gc
            edge_first[g, t] = gc[:3].astype(BF16)
            edge_last[g, t] = gc[TILE - 3 :].astype(BF16)
    to_after = copy_to(after, edge_last, north_g, s_halo.at[0], r_halo.at[0])
    to_before = copy_to(before, edge_first, south_g, s_halo.at[1], r_halo.at[1])
    to_after.start()
    to_before.start()

    emb_pair.wait_recv()
    emb_sum[...] = emb[...] + emb1[...]
    across = copy_to(at(dp, 1 - plane, z), emb_sum, emb2, s_e.at[1], r_e.at[1])
    across.start()

    @pl.loop(0, CG)
    def _(g):
        for j in range(7):

            def tile_taps(t, carry, j=j):
                gc = [gconv[g, t, a] for a in range(TILE)]
                total = list(carry)
                for r in range(14):
                    window = pad[g, t, r, 5 + j : 13 + j, :]
                    for i in range(7):
                        a = r - i
                        if 0 <= a < TILE:
                            total[i] = total[i] + window * gc[a]
                return tuple(total)

            sums = lax.fori_loop(
                0, CAP, tile_taps, tuple(jnp.zeros((8, 128), F32) for _ in range(7))
            )
            for i in range(7):
                kparts[g, i * 7 + j] = sums[i]

    for g in range(CG):
        lanes = slice(g * 128, g * 128 + 128)
        total = jnp.sum(kparts[g], axis=1)
        total = jnp.concatenate([total, jnp.zeros((15, 128), F32)], axis=0)
        for q in range(16):
            kgrads[q, :, lanes] = total[q * 4 : q * 4 + 4].astype(BF16)
    kpair = copy_to(partner, kgrads, kgot1, s1k.at[0], r1k.at[0])
    kpair.start()

    def from_tiles(i):
        return [gconv[g, i] for g in range(CG)]

    def from_edge(ref):
        return lambda i: [ref[g, i].astype(F32) for g in range(CG)]

    def back(t):
        spread(adj, t, pad_g, from_tiles, from_edge(north_g), from_edge(south_g))
        live = live_of(cnt, t)
        for g in range(CG):
            lanes = slice(g * 128, g * 128 + 128)
            rows = conv_tile(pad_g, taps, g, t, True)
            extra = pw[0, t] * cot[:, lanes] / TILE
            for a in range(TILE):
                g_out = live * (up[t, a, :, lanes].astype(F32) + extra)
                out[t, a, :, lanes] = (live * (g_out + rows[a])).astype(BF16)

    to_after.wait_recv()
    to_before.wait_recv()

    def kplane(q, slot, k):
        return copy_to(chunk_device(q), ksend2.at[q], kgot2.at[slot], s2k.at[k], r2k.at[slot])

    @pl.loop(0, CAP)
    def _(t):
        back(t)

        @pl.when(t == 0)
        def _():
            kpair.wait_recv()
            ksend2[...] = (kgrads[...].astype(F32) + kgot1[...].astype(F32)).astype(BF16)

            @pl.loop(1, 16)
            def _(k):
                kplane(lax.rem(spot + k, 16), spot, k).start()

            kgot2[spot] = ksend2[spot]

    across.wait_recv()
    emb_both = emb_sum[0:1] + emb2[0:1]
    high = emb_both.astype(BF16).astype(F32)
    mine = jnp.where(core == 0, high, emb_both - high)
    for h in range(HID // CHUNK):
        pair_of(h).wait_send()
    emb_pair.wait_send()
    kpair.wait_send()
    to_after.wait_send()
    to_before.wait_send()

    @pl.loop(1, 16)
    def _(k):
        q = lax.rem(spot + k, 16)
        kplane(q, q, k).wait_recv()
        for hh in range(2):
            copy_to(partner, send2.at[0, 0], got2.at[q, hh], s2.at[0, 0], r2.at[q, hh]).wait_recv()

    total = [got2[0, hh].astype(F32) for hh in range(2)]
    tail = kgot2[0].astype(F32)
    for q in range(1, 16):
        total = [total[hh] + got2[q, hh].astype(F32) for hh in range(2)]
        tail = tail + kgot2[q].astype(F32)

    for q in range(16):
        row = q % 8 * 3
        send3[q] = jnp.concatenate([total[q // 8][row : row + 3], tail, mine], axis=0).astype(BF16)

    def ring(q, slot, k):
        return copy_to(at(dp, plane, q), send3.at[q], got3.at[slot], s3.at[k], r3.at[slot])

    @pl.loop(1, 16)
    def _(k):
        ring(lax.rem(z + k, 16), z, k).start()

    got3[z] = send3[z]
    across.wait_send()
    for h in range(HID // CHUNK):

        @pl.loop(1, 8)
        def _(k):
            plane_of(h, k).wait_send()

        @pl.when(plane != h // 2)
        def _():
            plane_of(h, 0).wait_send()

    @pl.loop(1, 16)
    def _(k):
        q = lax.rem(spot + k, 16)
        kplane(q, q, k).wait_send()

    @pl.loop(1, 16)
    def _(k):
        q = lax.rem(z + k, 16)
        ring(q, q, k).wait_recv()

    total = got3[0].astype(F32)
    for q in range(1, 16):
        total = total + got3[q].astype(F32)

    send4[...] = total.astype(BF16)
    half[...] = jnp.broadcast_to(total[7:8], (8, C))

    def last(q, slot, k):
        return copy_to(chunk_device(q), send4, got4.at[slot], s4.at[k], r4.at[slot])

    @pl.loop(1, 16)
    def _(k):
        last(lax.rem(spot + k, 16), spot, k).start()

    swap = copy_to(partner, half, other, s5.at[0], r5.at[0])
    swap.start()
    got4[spot] = send4[...]

    @pl.loop(1, 16)
    def _(k):
        q = lax.rem(z + k, 16)
        ring(q, q, k).wait_send()

    swap.wait()
    emb_out[...] = half[...] + other[...]

    @pl.loop(1, 16)
    def _(k):
        q = lax.rem(spot + k, 16)
        last(q, q, k).wait()


def finish_kernel(out, got4, emb_got, emb, tiles, w_grad, k_grad):
    plane = lax.axis_index("space") // 32
    tiles[...] = out[...]
    emb[...] = emb_got[0:1]
    for d in range(8):
        w_grad[d * 3 : d * 3 + 3, :] = got4[d * 2 + plane, 0:3].astype(F32)
    for ij in range(49):
        row = got4[ij // 4, 3 + ij % 4 : 4 + ij % 4].astype(F32)
        k_grad[ij // 7, ij % 7 : ij % 7 + 1, :] = row


VMEM = pl.BlockSpec(memory_space=pltpu.VMEM)
SMEM = pl.BlockSpec(memory_space=pltpu.SMEM)
HBM = pl.BlockSpec(memory_space=pltpu.HBM)


def vmem(shape, dtype):
    return pltpu.VMEM(shape, dtype)


def per_device(
    tiles_in, upstream, pool_weight, slide_cot, adjacency, counts, kernel, norm_gain, w_in, w_out,
    layer_scale,
):
    own, up = tiles_in[0], upstream[0]
    spaces = lax.axis_size("space")
    struct = jax.ShapeDtypeStruct
    dma = pltpu.SemaphoreType.DMA
    edge = (CG, CAP, 3, TILE, 128)
    halo = (CAP, 3, TILE, C)
    blocks = (CG, CAP, TILE, TILE, 128)
    chunks = HID // CHUNK

    north, south = pl.pallas_call(
        functools.partial(halo_kernel, spaces),
        out_shape=(struct(halo, BF16), struct(halo, BF16)),
        in_specs=[HBM],
        out_specs=(HBM, HBM),
        scratch_shapes=[dma((2,)), dma((2,))],
        compiler_params=pltpu.CompilerParams(collective_id=0, has_side_effects=True),
        name="halo",
    )(own)

    out, got4, emb = pl.pallas_call(
        functools.partial(main_kernel, spaces),
        out_shape=(
            struct((CAP, TILE, TILE, C), BF16),
            struct((16, 8, C), BF16),
            struct((8, C), F32),
        ),
        in_specs=[SMEM] * 3 + [HBM] * 10,
        out_specs=(VMEM,) * 3,
        scratch_shapes=[
            vmem((CAP, TILE, TILE, C), BF16),
            vmem(halo, BF16),
            vmem(halo, BF16),
            vmem((CAP, TILE, TILE, C), BF16),
            vmem((1, C), F32),
            vmem((7, 7, C), F32),
            vmem((1, C), F32),
            vmem((1, C), F32),
            vmem((C, HID), BF16),
            vmem((HID, C), BF16),
            dma((10,)),
            vmem((CG, CAP, 14, 24, 128), F32),
            vmem((CG, CAP, 14, 24, 128), F32),
            vmem((CG, 49, 8, 128), F32),
            vmem(blocks, F32),
            vmem((CAP, 64, 128), F32),
            vmem((PIX, C), BF16),
            vmem((PIX, C), BF16),
            vmem((PIX, C), F32),
            vmem((PIX, HID), F32),
            vmem(blocks, F32),
            vmem((CG, 49, 8, 128), F32),
            vmem((2, chunks, 8, 24, C), BF16),
            vmem((chunks, 8, 24, C), BF16),
            vmem((chunks, 8, 24, C), BF16),
            vmem((16, 2, 24, C), BF16),
            vmem((16, 4, C), BF16),
            vmem((16, 4, C), BF16),
            vmem((16, 4, C), BF16),
            vmem((16, 4, C), BF16),
            vmem((8, C), F32),
            vmem((8, C), F32),
            vmem((8, C), F32),
            vmem((8, C), F32),
            vmem((16, 8, C), BF16),
            vmem((16, 8, C), BF16),
            vmem((8, C), BF16),
            vmem((8, C), F32),
            vmem((8, C), F32),
            vmem(edge, BF16),
            vmem(edge, BF16),
            vmem(edge, BF16),
            vmem(edge, BF16),
            dma((2,)), dma((2,)),
            dma((chunks,)), dma((chunks,)),
            dma((1,)), dma((1,)),
            dma((chunks, 8)), dma((16, 2)),
            dma((16,)), dma((16,)),
            dma((2,)), dma((2,)),
            dma((16,)), dma((16,)),
            dma((16,)), dma((16,)),
            dma((1,)), dma((1,)),
        ],
        compiler_params=pltpu.CompilerParams(
            collective_id=1, has_side_effects=True, vmem_limit_bytes=48 << 20
        ),
        name="main",
    )(
        pool_weight, adjacency[0], counts, own, north, south, up, slide_cot, kernel,
        norm_gain[None], layer_scale[None], w_in, w_out,
    )

    embedding, grad_tiles, w_grad, k_grad = pl.pallas_call(
        finish_kernel,
        out_shape=(
            struct((1, C), F32),
            struct((CAP, TILE, TILE, C), BF16),
            struct((24, C), F32),
            struct((7, 7, C), F32),
        ),
        in_specs=[VMEM] * 3,
        out_specs=(VMEM,) * 4,
        name="finish",
    )(out, got4, emb)
    return embedding, grad_tiles[None], w_grad, k_grad


def solution(mesh):
    return jax.shard_map(
        per_device,
        mesh=mesh,
        in_specs=(
            P("dp", "space", None, None, None),
            P("dp", "space", None, None, None),
            P("dp", "space"),
            P("dp", None),
            P("dp", "space", None),
            P("dp", "space"),
            P(),
            P(),
            P(),
            P(),
            P(),
        ),
        out_specs=(P("dp", None), P("dp", "space", None, None, None), P("space", None), P()),
        check_vma=False,
    )
```

```python
import contextlib
import functools

import jax
import jax.numpy as jnp
from jax import lax
from jax.experimental import pallas as pl
from jax.experimental.pallas import tpu as pltpu
from jax.sharding import PartitionSpec as P

MESH = pl.DeviceIdType.MESH
F32, BF16 = jnp.float32, jnp.bfloat16
sqrt_half = 0.7071067811865476
inv_root_two_pi = 0.3989422804014327

C, HID, CAP, TILE = 384, 1536, 4, 8
CG = C // 128
PIX = CAP * TILE * TILE
CHUNK = 384
VMEM_BYTES = 60 << 20
SCOPES = False


def scope(name):
    return jax.named_scope(name) if SCOPES else contextlib.nullcontext()


def spread(adj, t, pad, own, north, south):
    def entry(e):
        wanted = adj[t, e]
        return jnp.bitwise_and(jnp.maximum(wanted, 0), CAP - 1), wanted >= 0

    parts = []
    if own is not None:
        parts.append((3, 8, (own, 2), (own, None), (own, 3)))
    if north is not None:
        parts.append((0, 3, (north, 4), (north, 0), (north, 5)))
        parts.append((11, 3, (south, 6), (south, 1), (south, 7)))
    for row, rows, *columns in parts:
        for place, (source, e) in enumerate(columns):
            if e is None:
                groups = source(t)
            else:
                index, valid = entry(e)
                groups = [jnp.where(valid, g, 0.0) for g in source(index)]
            for g in range(CG):
                pad[g, t, row : row + rows, 8 * place : 8 * place + 8, :] = groups[g]


def conv_tile(pad, taps, g, t, flip):
    total = [None] * TILE
    for j in range(7):
        column = [taps[g, 48 - (i * 7 + j) if flip else i * 7 + j] for i in range(7)]
        for r in range(14):
            window = pad[g, t, r, 5 + j : 13 + j, :]
            for i in range(7):
                a = r - i
                if 0 <= a < TILE:
                    term = window * column[i]
                    total[a] = term if total[a] is None else total[a] + term
    return total


def split_groups(value):
    return [value[..., g * 128 : (g + 1) * 128] for g in range(CG)]


def live_of(cnt, t):
    return jnp.where(t < cnt[0, 0], 1.0, 0.0).astype(F32)


def grad_out_of(up, pw, cot, live, t):
    extra = pw[0, t] * cot[...] / TILE
    return live * (up[t].astype(F32) + extra[None])


def load_taps(ker, taps):
    for ij in range(49):
        row = ker[ij // 7, ij % 7 : ij % 7 + 1, :]
        for g in range(CG):
            taps[g, ij] = jnp.broadcast_to(row[:, g * 128 : (g + 1) * 128], (8, 128))


def copy_to(device, src, dst, send, recv):
    return pltpu.make_async_remote_copy(
        src_ref=src, dst_ref=dst, send_sem=send, recv_sem=recv,
        device_id=device, device_id_type=MESH,
    )


def greet(device):
    pl.semaphore_signal(
        pltpu.get_barrier_semaphore(), inc=1, device_id=device, device_id_type=MESH
    )


def main_kernel(
    spaces,
    pw, adj, cnt,
    own_in, up_in, cot_in, ker_in, gain_in, scale_in, w_in_in, w_out_in,
    out_hbm, got4, emb_hbm,
    out, emb_out, out_sems, own, north, south, up, cot, ker, gain, scale, w_in, w_out, load_sems,
    pad, pad_g, taps, normed, inv, lifted, gmix, glift, slope, gacts, order, gconv, kparts,
    grads, got1, send2, got2, kgrads, kgot1, ksend2, kgot2,
    emb, emb1, emb_sum, emb2, send3, got3, send4, half, other,
    edge_first, edge_last, north_g, south_g,
    s_fore, r_fore, s_halo, r_halo, s1, r1, s1k, r1k, s2, r2, s2k, r2k, s_e, r_e, s3, r3, s4, r4, s5, r5,
):
    dp, space = lax.axis_index("dp"), lax.axis_index("space")
    core = lax.rem(space, 2)
    z = lax.rem(space // 2, 16)
    plane = space // 32
    spot = dp * 2 + plane

    def at(d, p, zz):
        return (d, (p * 16 + zz) * 2 + core)

    def chunk_device(q):
        return at(q // 2, lax.rem(q, 2), z)

    partner = (dp, space + 1 - 2 * core)
    before = (dp, lax.rem(space + spaces - 1, spaces))
    after = (dp, lax.rem(space + 1, spaces))

    loads = {}
    sources = dict(
        own=(own_in, own), ker=(ker_in, ker), up=(up_in, up), cot=(cot_in, cot),
        scale=(scale_in, scale), w_out=(w_out_in, w_out), gain=(gain_in, gain), w_in=(w_in_in, w_in),
    )
    for n, (name, (src, dst)) in enumerate(sources.items()):
        loads[name] = pltpu.make_async_copy(src, dst, load_sems.at[n])
        loads[name].start()

    with scope("greet"):
        greet(before)
        greet(after)

        @pl.loop(1, 16)
        def _(k):
            greet(at(dp, plane, lax.rem(z + k, 16)))
            greet(chunk_device(lax.rem(spot + k, 16)))

    with scope("gmix"):
        for name in ("own", "up", "cot", "scale"):
            loads[name].wait()
        scale_row = scale[...].reshape(1, C)
        emb_own = jnp.zeros((1, C), F32)
        for t in range(CAP):
            live = live_of(cnt, t)
            here = slice(t * 64, t * 64 + 64)
            g_out = grad_out_of(up, pw, cot, live, t)
            gmix[here, :] = (g_out * scale_row[None]).astype(BF16).reshape(64, C)
            weight = live * pw[0, t]
            emb_own = emb_own + weight * jnp.sum(
                own[t].astype(F32).reshape(64, C), axis=0, keepdims=True
            )

    with scope("barrier"):
        pl.semaphore_wait(pltpu.get_barrier_semaphore(), 32)
    down = copy_to(after, own.at[:, TILE - 3 :], north, s_fore.at[0], r_fore.at[0])
    upward = copy_to(before, own.at[:, :3], south, s_fore.at[1], r_fore.at[1])
    down.start()
    upward.start()

    def groups_of(ref):
        return lambda i: split_groups(ref[i].astype(F32))

    with scope("under_halo"):
        loads["ker"].wait()
        load_taps(ker, taps)

        @pl.loop(0, CAP)
        def _(t):
            spread(adj, t, pad, groups_of(own), None, None)

        d = lax.broadcasted_iota(jnp.int32, (8, CHUNK), 1)
        d_core = jnp.where(d >= 192, 1, 0)
        d = d - 192 * d_core
        d_dp = jnp.zeros_like(d)
        for m in range(1, 8):
            d_dp = d_dp + jnp.where(d >= 24 * m, 1, 0)
        d = d - 24 * d_dp
        d_z = jnp.zeros_like(d)
        for m in range(1, 8):
            d_z = d_z + jnp.where(d >= 3 * m, 1, 0)
        d = d - 3 * d_z
        source = d_z * 48 + d_core * 24 + d_dp * 3 + d
        rows = lax.broadcasted_iota(jnp.int32, (CHUNK, CHUNK), 0)
        order[...] = jnp.where(rows == source[0:1], 1.0, 0.0).astype(BF16)
        loads["w_out"].wait()
        for h in range(HID // CHUNK):
            here = slice(h * CHUNK, (h + 1) * CHUNK)
            gacts[:, here] = lax.dot_general(
                gmix[...], w_out[here, :], (((1,), (1,)), ((), ())), preferred_element_type=F32
            )

    with scope("halo_wait"):
        down.wait_recv()
        upward.wait_recv()

    with scope("spread"):

        @pl.loop(0, CAP)
        def _(t):
            spread(adj, t, pad, None, groups_of(north), groups_of(south))

    with scope("conv"):

        @pl.loop(0, CAP)
        def _(t):
            @pl.loop(0, CG)
            def _(g):
                rows = conv_tile(pad, taps, g, t, False)
                for a in range(TILE):
                    normed[g, t, a] = rows[a]

    with scope("norm"):
        loads["gain"].wait()
        gain_row = gain[...].reshape(1, C)
        for t in range(CAP):
            x = [normed[g, t].reshape(64, 128) for g in range(CG)]
            mean = jnp.sum(x[0] + x[1] + x[2], axis=-1, keepdims=True) / C
            x = [v - mean for v in x]
            var = jnp.sum(x[0] * x[0] + x[1] * x[1] + x[2] * x[2], axis=-1, keepdims=True) / C
            istd = jnp.broadcast_to(lax.rsqrt(var + 1e-06), (64, 128))
            inv[t] = istd
            here = slice(t * 64, t * 64 + 64)
            for g in range(CG):
                lanes = slice(g * 128, g * 128 + 128)
                n = x[g] * istd
                normed[g, t] = n.reshape(TILE, TILE, 128)
                lifted[here, lanes] = (n * gain_row[:, lanes]).astype(BF16)
        loads["w_in"].wait()

    def pair_of(h):
        return copy_to(partner, grads.at[1 - core, h], got1.at[h], s1.at[h], r1.at[h])

    def plane_of(h, k):
        to = lax.rem(dp + k, 8)
        return copy_to(
            at(to, h // 2, z), send2.at[h, to], got2.at[spot, h % 2], s2.at[h, k],
            r2.at[spot, h % 2],
        )

    def pass_on(h):
        pair_of(h).wait_recv()
        send2[h] = (grads[core, h].astype(F32) + got1[h].astype(F32)).astype(BF16)

        @pl.loop(1, 8)
        def _(k):
            plane_of(h, k).start()

        @pl.when(plane == h // 2)
        def _():
            got2[spot, h % 2] = send2[h, dp]

        @pl.when(plane != h // 2)
        def _():
            plane_of(h, 0).start()

    mixed = jnp.zeros((8, C), F32)
    for h in range(HID // CHUNK):
        here = slice(h * CHUNK, (h + 1) * CHUNK)
        pre = jnp.dot(lifted[...], w_in[:, here], preferred_element_type=F32)
        cdf = 0.5 * (1.0 + lax.erf(pre * sqrt_half))
        act = (pre * cdf).astype(BF16)
        density = jnp.exp(-0.5 * pre * pre) * inv_root_two_pi
        slope[:, here] = cdf + pre * density
        sent = jnp.dot(act, order[...], preferred_element_type=F32).astype(BF16)
        gw = lax.dot_general(
            sent, gmix[...], (((0,), (0,)), ((), ())), preferred_element_type=F32
        ).astype(BF16)
        for c in range(2):
            for m in range(8):
                grads[c, h, m] = gw[(c * 8 + m) * 24 : (c * 8 + m) * 24 + 24]
        pair_of(h).start()
        pooled = jnp.zeros((1, CHUNK), F32)
        for t in range(CAP):
            weight = live_of(cnt, t) * pw[0, t]
            pooled = pooled + weight * jnp.sum(
                act[t * 64 : t * 64 + 64].astype(F32), axis=0, keepdims=True
            )
        high = pooled.astype(BF16)
        rest = pooled - high.astype(F32)
        middle = rest.astype(BF16)
        low = (rest - middle.astype(F32)).astype(BF16)
        three = jnp.concatenate([high, middle, low, jnp.zeros((5, CHUNK), BF16)], axis=0)
        mixed = mixed + jnp.dot(three, w_out[here, :], preferred_element_type=F32)
        if h > 0:
            pass_on(h - 1)
    mix = jnp.sum(mixed, axis=0, keepdims=True)
    emb[...] = jnp.broadcast_to((emb_own + scale_row * mix) / TILE, (8, C))
    emb_pair = copy_to(partner, emb, emb1, s_e.at[0], r_e.at[0])
    emb_pair.start()

    for h in range(HID // CHUNK):
        here = slice(h * CHUNK, (h + 1) * CHUNK)
        gpre = (gacts[:, here] * slope[:, here]).astype(BF16)
        gl = lax.dot_general(
            gpre, w_in[:, here], (((1,), (1,)), ((), ())), preferred_element_type=F32
        )
        if h == 0:
            glift[...] = gl
            pass_on(HID // CHUNK - 1)
        else:
            glift[...] += gl

    for t in range(CAP):
        here = slice(t * 64, t * 64 + 64)
        gn = [glift[here, g * 128 : g * 128 + 128] * gain_row[:, g * 128 : g * 128 + 128] for g in range(CG)]
        n = [normed[g, t].reshape(64, 128) for g in range(CG)]
        m1 = jnp.sum(gn[0] + gn[1] + gn[2], axis=-1, keepdims=True) / C
        m2 = jnp.sum(gn[0] * n[0] + gn[1] * n[1] + gn[2] * n[2], axis=-1, keepdims=True) / C
        for g in range(CG):
            gc = (inv[t] * (gn[g] - m1 - n[g] * m2)).reshape(TILE, TILE, 128)
            gconv[g, t] = gc
            edge_first[g, t] = gc[:3].astype(BF16)
            edge_last[g, t] = gc[TILE - 3 :].astype(BF16)
    to_after = copy_to(after, edge_last, north_g, s_halo.at[0], r_halo.at[0])
    to_before = copy_to(before, edge_first, south_g, s_halo.at[1], r_halo.at[1])
    to_after.start()
    to_before.start()

    emb_pair.wait_recv()
    emb_sum[...] = emb[...] + emb1[...]
    across = copy_to(at(dp, 1 - plane, z), emb_sum, emb2, s_e.at[1], r_e.at[1])
    across.start()

    @pl.loop(0, CG)
    def _(g):
        for j in range(7):

            def tile_taps(t, carry, j=j):
                gc = [gconv[g, t, a] for a in range(TILE)]
                total = list(carry)
                for r in range(14):
                    window = pad[g, t, r, 5 + j : 13 + j, :]
                    for i in range(7):
                        a = r - i
                        if 0 <= a < TILE:
                            total[i] = total[i] + window * gc[a]
                return tuple(total)

            sums = lax.fori_loop(
                0, CAP, tile_taps, tuple(jnp.zeros((8, 128), F32) for _ in range(7))
            )
            for i in range(7):
                kparts[g, i * 7 + j] = sums[i]

    for g in range(CG):
        lanes = slice(g * 128, g * 128 + 128)
        total = jnp.sum(kparts[g], axis=1)
        total = jnp.concatenate([total, jnp.zeros((15, 128), F32)], axis=0)
        for q in range(16):
            kgrads[q, :, lanes] = total[q * 4 : q * 4 + 4].astype(BF16)
    kpair = copy_to(partner, kgrads, kgot1, s1k.at[0], r1k.at[0])
    kpair.start()

    def from_tiles(i):
        return [gconv[g, i] for g in range(CG)]

    def from_edge(ref):
        return lambda i: [ref[g, i].astype(F32) for g in range(CG)]

    def back(t):
        spread(adj, t, pad_g, from_tiles, from_edge(north_g), from_edge(south_g))
        live = live_of(cnt, t)
        for g in range(CG):
            lanes = slice(g * 128, g * 128 + 128)
            rows = conv_tile(pad_g, taps, g, t, True)
            extra = pw[0, t] * cot[:, lanes] / TILE
            for a in range(TILE):
                g_out = live * (up[t, a, :, lanes].astype(F32) + extra)
                out[t, a, :, lanes] = (live * (g_out + rows[a])).astype(BF16)

    to_after.wait_recv()
    to_before.wait_recv()

    def kplane(q, slot, k):
        return copy_to(chunk_device(q), ksend2.at[q], kgot2.at[slot], s2k.at[k], r2k.at[slot])

    @pl.loop(0, CAP)
    def _(t):
        back(t)

        @pl.when(t == 0)
        def _():
            kpair.wait_recv()
            ksend2[...] = (kgrads[...].astype(F32) + kgot1[...].astype(F32)).astype(BF16)

            @pl.loop(1, 16)
            def _(k):
                kplane(lax.rem(spot + k, 16), spot, k).start()

            kgot2[spot] = ksend2[spot]

    out_copy = pltpu.make_async_copy(out, out_hbm, out_sems.at[0])
    out_copy.start()
    down.wait_send()
    upward.wait_send()
    across.wait_recv()
    emb_both = emb_sum[0:1] + emb2[0:1]
    high = emb_both.astype(BF16).astype(F32)
    mine = jnp.where(core == 0, high, emb_both - high)
    for h in range(HID // CHUNK):
        pair_of(h).wait_send()
    emb_pair.wait_send()
    kpair.wait_send()
    to_after.wait_send()
    to_before.wait_send()

    @pl.loop(1, 16)
    def _(k):
        q = lax.rem(spot + k, 16)
        kplane(q, q, k).wait_recv()
        for hh in range(2):
            copy_to(partner, send2.at[0, 0], got2.at[q, hh], s2.at[0, 0], r2.at[q, hh]).wait_recv()

    total = [got2[0, hh].astype(F32) for hh in range(2)]
    tail = kgot2[0].astype(F32)
    for q in range(1, 16):
        total = [total[hh] + got2[q, hh].astype(F32) for hh in range(2)]
        tail = tail + kgot2[q].astype(F32)

    for q in range(16):
        row = q % 8 * 3
        send3[q] = jnp.concatenate([total[q // 8][row : row + 3], tail, mine], axis=0).astype(BF16)

    def ring(q, slot, k):
        return copy_to(at(dp, plane, q), send3.at[q], got3.at[slot], s3.at[k], r3.at[slot])

    @pl.loop(1, 16)
    def _(k):
        ring(lax.rem(z + k, 16), z, k).start()

    got3[z] = send3[z]
    across.wait_send()
    for h in range(HID // CHUNK):

        @pl.loop(1, 8)
        def _(k):
            plane_of(h, k).wait_send()

        @pl.when(plane != h // 2)
        def _():
            plane_of(h, 0).wait_send()

    @pl.loop(1, 16)
    def _(k):
        q = lax.rem(spot + k, 16)
        kplane(q, q, k).wait_send()

    @pl.loop(1, 16)
    def _(k):
        q = lax.rem(z + k, 16)
        ring(q, q, k).wait_recv()

    total = got3[0].astype(F32)
    for q in range(1, 16):
        total = total + got3[q].astype(F32)

    send4[...] = total.astype(BF16)
    half[...] = jnp.broadcast_to(total[7:8], (8, C))

    def last(q, slot, k):
        return copy_to(chunk_device(q), send4, got4.at[slot], s4.at[k], r4.at[slot])

    @pl.loop(1, 16)
    def _(k):
        last(lax.rem(spot + k, 16), spot, k).start()

    swap = copy_to(partner, half, other, s5.at[0], r5.at[0])
    swap.start()
    own_copy = pltpu.make_async_copy(send4, got4.at[spot], out_sems.at[1])
    own_copy.start()

    @pl.loop(1, 16)
    def _(k):
        q = lax.rem(z + k, 16)
        ring(q, q, k).wait_send()

    swap.wait()
    emb_out[...] = half[...] + other[...]
    emb_copy = pltpu.make_async_copy(emb_out, emb_hbm, out_sems.at[2])
    emb_copy.start()
    out_copy.wait()
    own_copy.wait()
    emb_copy.wait()

    @pl.loop(1, 16)
    def _(k):
        q = lax.rem(spot + k, 16)
        last(q, q, k).wait()


def finish_kernel(out, got4_in, emb_in, emb, tiles, w_grad, k_grad, got4, emb_got, sems):
    plane = lax.axis_index("space") // 32
    loads = [
        pltpu.make_async_copy(got4_in, got4, sems.at[0]),
        pltpu.make_async_copy(emb_in, emb_got, sems.at[1]),
        pltpu.make_async_copy(out, tiles, sems.at[2]),
    ]
    for load in loads:
        load.start()
    loads[0].wait()
    for d in range(8):
        w_grad[d * 3 : d * 3 + 3, :] = got4[d * 2 + plane, 0:3].astype(F32)
    for ij in range(49):
        row = got4[ij // 4, 3 + ij % 4 : 4 + ij % 4].astype(F32)
        k_grad[ij // 7, ij % 7 : ij % 7 + 1, :] = row
    loads[1].wait()
    emb[...] = emb_got[0:1]
    loads[2].wait()


VMEM = pl.BlockSpec(memory_space=pltpu.VMEM)
SMEM = pl.BlockSpec(memory_space=pltpu.SMEM)
HBM = pl.BlockSpec(memory_space=pltpu.HBM)


def vmem(shape, dtype):
    return pltpu.VMEM(shape, dtype)


def per_device(
    tiles_in, upstream, pool_weight, slide_cot, adjacency, counts, kernel, norm_gain, w_in, w_out,
    layer_scale,
):
    own, up = tiles_in[0], upstream[0]
    spaces = lax.axis_size("space")
    struct = jax.ShapeDtypeStruct
    dma = pltpu.SemaphoreType.DMA
    edge = (CG, CAP, 3, TILE, 128)
    halo = (CAP, 3, TILE, C)
    blocks = (CG, CAP, TILE, TILE, 128)
    chunks = HID // CHUNK

    out, got4, emb = pl.pallas_call(
        functools.partial(main_kernel, spaces),
        out_shape=(
            struct((CAP, TILE, TILE, C), BF16),
            struct((16, 8, C), BF16),
            struct((8, C), F32),
        ),
        in_specs=[SMEM] * 3 + [HBM] * 8,
        out_specs=(HBM,) * 3,
        scratch_shapes=[
            vmem((CAP, TILE, TILE, C), BF16),
            vmem((8, C), F32),
            dma((3,)),
            vmem((CAP, TILE, TILE, C), BF16),
            vmem(halo, BF16),
            vmem(halo, BF16),
            vmem((CAP, TILE, TILE, C), BF16),
            vmem((1, C), F32),
            vmem((7, 7, C), F32),
            vmem((C,), F32),
            vmem((C,), F32),
            vmem((C, HID), BF16),
            vmem((HID, C), BF16),
            dma((8,)),
            vmem((CG, CAP, 14, 24, 128), F32),
            vmem((CG, CAP, 14, 24, 128), F32),
            vmem((CG, 49, 8, 128), F32),
            vmem(blocks, F32),
            vmem((CAP, 64, 128), F32),
            vmem((PIX, C), BF16),
            vmem((PIX, C), BF16),
            vmem((PIX, C), F32),
            vmem((PIX, HID), F32),
            vmem((PIX, HID), F32),
            vmem((CHUNK, CHUNK), BF16),
            vmem(blocks, F32),
            vmem((CG, 49, 8, 128), F32),
            vmem((2, chunks, 8, 24, C), BF16),
            vmem((chunks, 8, 24, C), BF16),
            vmem((chunks, 8, 24, C), BF16),
            vmem((16, 2, 24, C), BF16),
            vmem((16, 4, C), BF16),
            vmem((16, 4, C), BF16),
            vmem((16, 4, C), BF16),
            vmem((16, 4, C), BF16),
            vmem((8, C), F32),
            vmem((8, C), F32),
            vmem((8, C), F32),
            vmem((8, C), F32),
            vmem((16, 8, C), BF16),
            vmem((16, 8, C), BF16),
            vmem((8, C), BF16),
            vmem((8, C), F32),
            vmem((8, C), F32),
            vmem(edge, BF16),
            vmem(edge, BF16),
            vmem(edge, BF16),
            vmem(edge, BF16),
            dma((2,)), dma((2,)),
            dma((2,)), dma((2,)),
            dma((chunks,)), dma((chunks,)),
            dma((1,)), dma((1,)),
            dma((chunks, 8)), dma((16, 2)),
            dma((16,)), dma((16,)),
            dma((2,)), dma((2,)),
            dma((16,)), dma((16,)),
            dma((16,)), dma((16,)),
            dma((1,)), dma((1,)),
        ],
        compiler_params=pltpu.CompilerParams(
            collective_id=0, has_side_effects=True, vmem_limit_bytes=VMEM_BYTES
        ),
        name="main",
    )(
        pool_weight, adjacency[0], counts, own, up, slide_cot, kernel, norm_gain, layer_scale, w_in,
        w_out,
    )

    embedding, grad_tiles, w_grad, k_grad = pl.pallas_call(
        finish_kernel,
        out_shape=(
            struct((1, C), F32),
            struct((CAP, TILE, TILE, C), BF16),
            struct((24, C), F32),
            struct((7, 7, C), F32),
        ),
        in_specs=[HBM] * 3,
        out_specs=(VMEM, HBM, VMEM, VMEM),
        scratch_shapes=[vmem((16, 8, C), BF16), vmem((8, C), F32), dma((3,))],
        name="finish",
    )(out, got4, emb)
    return embedding, grad_tiles[None], w_grad, k_grad


def solution(mesh):
    return jax.shard_map(
        per_device,
        mesh=mesh,
        in_specs=(
            P("dp", "space", None, None, None),
            P("dp", "space", None, None, None),
            P("dp", "space"),
            P("dp", None),
            P("dp", "space", None),
            P("dp", "space"),
            P(),
            P(),
            P(),
            P(),
            P(),
        ),
        out_specs=(P("dp", None), P("dp", "space", None, None, None), P("space", None), P()),
        check_vma=False,
    )
```

```python
import contextlib
import functools

import jax
import jax.numpy as jnp
from jax import lax
from jax.experimental import pallas as pl
from jax.experimental.pallas import tpu as pltpu
from jax.sharding import PartitionSpec as P

MESH = pl.DeviceIdType.MESH
F32, BF16 = jnp.float32, jnp.bfloat16
sqrt_half = 0.7071067811865476
inv_root_two_pi = 0.3989422804014327

C, HID, CAP, TILE = 384, 1536, 4, 8
CG = C // 128
PIX = CAP * TILE * TILE
CHUNK = 384
VMEM_BYTES = 60 << 20
SCOPES = False


def scope(name):
    return jax.named_scope(name) if SCOPES else contextlib.nullcontext()


def spread(adj, t, pad, own, north, south):
    def entry(e):
        wanted = adj[t, e]
        return jnp.bitwise_and(jnp.maximum(wanted, 0), CAP - 1), wanted >= 0

    parts = []
    if own is not None:
        parts.append((3, 8, (own, 2), (own, None), (own, 3)))
    if north is not None:
        parts.append((0, 3, (north, 4), (north, 0), (north, 5)))
        parts.append((11, 3, (south, 6), (south, 1), (south, 7)))
    for row, rows, *columns in parts:
        for place, (source, e) in enumerate(columns):
            if e is None:
                groups = source(t)
            else:
                index, valid = entry(e)
                groups = [jnp.where(valid, g, 0.0) for g in source(index)]
            for g in range(CG):
                pad[g, t, row : row + rows, 8 * place : 8 * place + 8, :] = groups[g]


def conv_tile(pad, taps, g, t, flip, rows=range(14), start=None):
    total = list(start) if start is not None else [None] * TILE
    for j in range(7):
        column = [taps[g, 48 - (i * 7 + j) if flip else i * 7 + j] for i in range(7)]
        for r in rows:
            window = pad[g, t, r, 5 + j : 13 + j, :]
            for i in range(7):
                a = r - i
                if 0 <= a < TILE:
                    term = window * column[i]
                    total[a] = term if total[a] is None else total[a] + term
    return total


OWN_ROWS = range(3, 11)
EDGE_ROWS = (0, 1, 2, 11, 12, 13)
RING_ORDER = (8, 7, 9, 6, 10, 5, 11, 4, 12, 3, 13, 2, 14, 1, 15)
PLANE_ORDER = (
    (2, 2), (2, 1), (2, 3), (1, 2), (3, 2), (2, 0), (0, 2), (1, 1), (1, 3), (3, 1), (3, 3), (0, 1),
    (0, 3), (1, 0), (3, 0),
)
DP_ORDER = (4, 5, 3, 2, 6, 7, 1)


def wrapped(value, size):
    return jnp.where(value >= size, value - size, value)


def split_groups(value):
    return [value[..., g * 128 : (g + 1) * 128] for g in range(CG)]


def live_of(cnt, t):
    return jnp.where(t < cnt[0, 0], 1.0, 0.0).astype(F32)


def grad_out_of(up, pw, cot, live, t):
    extra = pw[0, t] * cot[...] / TILE
    return live * (up[t].astype(F32) + extra[None])


def load_taps(ker, taps):
    for ij in range(49):
        row = ker[ij // 7, ij % 7 : ij % 7 + 1, :]
        for g in range(CG):
            taps[g, ij] = jnp.broadcast_to(row[:, g * 128 : (g + 1) * 128], (8, 128))


def copy_to(device, src, dst, send, recv):
    return pltpu.make_async_remote_copy(
        src_ref=src, dst_ref=dst, send_sem=send, recv_sem=recv,
        device_id=device, device_id_type=MESH,
    )


def greet(device):
    pl.semaphore_signal(
        pltpu.get_barrier_semaphore(), inc=1, device_id=device, device_id_type=MESH
    )


def main_kernel(
    spaces,
    pw, adj, cnt,
    own_in, up_in, cot_in, ker_in, gain_in, scale_in, w_in_in, w_out_in,
    out_hbm, got4, emb_hbm,
    out, emb_out, out_sems, own, north, south, up, cot, ker, gain, scale, w_in, w_out, load_sems,
    pad, pad_g, taps, normed, inv, lifted, gmix, glift, slope, gacts, order, gconv, kparts,
    grads, got1, send2, got2, kgrads, kgot1, ksend2, kgot2,
    emb, emb1, emb_sum, emb2, send3, got3, send4, half, other,
    edge_first, edge_last, north_g, south_g,
    s_fore, r_fore, s_halo, r_halo, s1, r1, s1k, r1k, s2, r2, s2k, r2k, s_e, r_e, s3, r3, s4, r4, s5, r5,
):
    dp, space = lax.axis_index("dp"), lax.axis_index("space")
    core = lax.rem(space, 2)
    z = lax.rem(space // 2, 16)
    plane = space // 32
    spot = dp * 2 + plane

    def at(d, p, zz):
        return (d, (p * 16 + zz) * 2 + core)

    px, py = dp // 2, lax.rem(dp, 2) * 2 + plane

    def plane_device(dx, dy):
        x, y = wrapped(px + dx, 4), wrapped(py + dy, 4)
        return x * 4 + y, at(x * 2 + y // 2, lax.rem(y, 2), z)

    partner = (dp, space + 1 - 2 * core)
    before = (dp, lax.rem(space + spaces - 1, spaces))
    after = (dp, lax.rem(space + 1, spaces))

    loads = {}
    sources = dict(
        own=(own_in, own), ker=(ker_in, ker), up=(up_in, up), cot=(cot_in, cot),
        scale=(scale_in, scale), w_out=(w_out_in, w_out), gain=(gain_in, gain), w_in=(w_in_in, w_in),
    )
    for n, (name, (src, dst)) in enumerate(sources.items()):
        loads[name] = pltpu.make_async_copy(src, dst, load_sems.at[n])
        loads[name].start()

    with scope("greet"):
        greet(before)
        greet(after)

        for k in RING_ORDER:
            greet(at(dp, plane, wrapped(z + k, 16)))
        for dx, dy in PLANE_ORDER:
            greet(plane_device(dx, dy)[1])

    with scope("gmix"):
        for name in ("own", "up", "cot", "scale"):
            loads[name].wait()
        scale_row = scale[...].reshape(1, C)
        emb_own = jnp.zeros((1, C), F32)
        for t in range(CAP):
            live = live_of(cnt, t)
            here = slice(t * 64, t * 64 + 64)
            g_out = grad_out_of(up, pw, cot, live, t)
            gmix[here, :] = (g_out * scale_row[None]).astype(BF16).reshape(64, C)
            weight = live * pw[0, t]
            emb_own = emb_own + weight * jnp.sum(
                own[t].astype(F32).reshape(64, C), axis=0, keepdims=True
            )

    with scope("barrier"):
        pl.semaphore_wait(pltpu.get_barrier_semaphore(), 32)
    down = copy_to(after, own.at[:, TILE - 3 :], north, s_fore.at[0], r_fore.at[0])
    upward = copy_to(before, own.at[:, :3], south, s_fore.at[1], r_fore.at[1])
    down.start()
    upward.start()

    def groups_of(ref):
        return lambda i: split_groups(ref[i].astype(F32))

    with scope("under_halo"):
        loads["ker"].wait()
        load_taps(ker, taps)

        @pl.loop(0, CAP)
        def _(t):
            spread(adj, t, pad, groups_of(own), None, None)

        d = lax.broadcasted_iota(jnp.int32, (8, CHUNK), 1)
        d_core = jnp.where(d >= 192, 1, 0)
        d = d - 192 * d_core
        d_dp = jnp.zeros_like(d)
        for m in range(1, 8):
            d_dp = d_dp + jnp.where(d >= 24 * m, 1, 0)
        d = d - 24 * d_dp
        d_z = jnp.zeros_like(d)
        for m in range(1, 8):
            d_z = d_z + jnp.where(d >= 3 * m, 1, 0)
        d = d - 3 * d_z
        source = d_z * 48 + d_core * 24 + d_dp * 3 + d
        rows = lax.broadcasted_iota(jnp.int32, (CHUNK, CHUNK), 0)
        order[...] = jnp.where(rows == source[0:1], 1.0, 0.0).astype(BF16)
        loads["w_out"].wait()

        @pl.loop(0, CAP)
        def _(t):
            @pl.loop(0, CG)
            def _(g):
                rows = conv_tile(pad, taps, g, t, False, OWN_ROWS)
                for a in range(TILE):
                    normed[g, t, a] = rows[a]

        for h in range(HID // CHUNK):
            here = slice(h * CHUNK, (h + 1) * CHUNK)
            gacts[:, here] = lax.dot_general(
                gmix[...], w_out[here, :], (((1,), (1,)), ((), ())), preferred_element_type=F32
            )

    with scope("halo_wait"):
        down.wait_recv()
        upward.wait_recv()

    with scope("spread"):

        @pl.loop(0, CAP)
        def _(t):
            spread(adj, t, pad, None, groups_of(north), groups_of(south))

    with scope("conv"):

        @pl.loop(0, CAP)
        def _(t):
            @pl.loop(0, CG)
            def _(g):
                start = [normed[g, t, a] for a in range(TILE)]
                rows = conv_tile(pad, taps, g, t, False, EDGE_ROWS, start)
                for a in range(TILE):
                    normed[g, t, a] = rows[a]

    with scope("norm"):
        loads["gain"].wait()
        gain_row = gain[...].reshape(1, C)
        for t in range(CAP):
            x = [normed[g, t].reshape(64, 128) for g in range(CG)]
            mean = jnp.sum(x[0] + x[1] + x[2], axis=-1, keepdims=True) / C
            x = [v - mean for v in x]
            var = jnp.sum(x[0] * x[0] + x[1] * x[1] + x[2] * x[2], axis=-1, keepdims=True) / C
            istd = jnp.broadcast_to(lax.rsqrt(var + 1e-06), (64, 128))
            inv[t] = istd
            here = slice(t * 64, t * 64 + 64)
            for g in range(CG):
                lanes = slice(g * 128, g * 128 + 128)
                n = x[g] * istd
                normed[g, t] = n.reshape(TILE, TILE, 128)
                lifted[here, lanes] = (n * gain_row[:, lanes]).astype(BF16)
        loads["w_in"].wait()

    def pair_of(h):
        return copy_to(partner, grads.at[1 - core, h], got1.at[h], s1.at[h], r1.at[h])

    def plane_of(h, k):
        to = wrapped(dp + k, 8)
        return copy_to(
            at(to, h // 2, z), send2.at[h, to], got2.at[spot, h % 2], s2.at[h, k],
            r2.at[spot, h % 2],
        )

    def pass_on(h):
        pair_of(h).wait_recv()
        send2[h] = (grads[core, h].astype(F32) + got1[h].astype(F32)).astype(BF16)

        for k in DP_ORDER:
            plane_of(h, k).start()

        @pl.when(plane == h // 2)
        def _():
            got2[spot, h % 2] = send2[h, dp]

        @pl.when(plane != h // 2)
        def _():
            plane_of(h, 0).start()

    mixed = jnp.zeros((8, C), F32)
    for h in range(HID // CHUNK):
        here = slice(h * CHUNK, (h + 1) * CHUNK)
        pre = jnp.dot(lifted[...], w_in[:, here], preferred_element_type=F32)
        cdf = 0.5 * (1.0 + lax.erf(pre * sqrt_half))
        act = (pre * cdf).astype(BF16)
        density = jnp.exp(-0.5 * pre * pre) * inv_root_two_pi
        slope[:, here] = cdf + pre * density
        sent = jnp.dot(act, order[...], preferred_element_type=F32).astype(BF16)
        gw = lax.dot_general(
            sent, gmix[...], (((0,), (0,)), ((), ())), preferred_element_type=F32
        ).astype(BF16)
        for c in range(2):
            for m in range(8):
                grads[c, h, m] = gw[(c * 8 + m) * 24 : (c * 8 + m) * 24 + 24]
        pair_of(h).start()
        pooled = jnp.zeros((1, CHUNK), F32)
        for t in range(CAP):
            weight = live_of(cnt, t) * pw[0, t]
            pooled = pooled + weight * jnp.sum(
                act[t * 64 : t * 64 + 64].astype(F32), axis=0, keepdims=True
            )
        high = pooled.astype(BF16)
        rest = pooled - high.astype(F32)
        middle = rest.astype(BF16)
        low = (rest - middle.astype(F32)).astype(BF16)
        three = jnp.concatenate([high, middle, low, jnp.zeros((5, CHUNK), BF16)], axis=0)
        mixed = mixed + jnp.dot(three, w_out[here, :], preferred_element_type=F32)
        if h > 0:
            pass_on(h - 1)
    mix = jnp.sum(mixed, axis=0, keepdims=True)
    emb[...] = jnp.broadcast_to((emb_own + scale_row * mix) / TILE, (8, C))
    emb_pair = copy_to(partner, emb, emb1, s_e.at[0], r_e.at[0])
    emb_pair.start()

    for h in range(HID // CHUNK):
        here = slice(h * CHUNK, (h + 1) * CHUNK)
        gpre = (gacts[:, here] * slope[:, here]).astype(BF16)
        gl = lax.dot_general(
            gpre, w_in[:, here], (((1,), (1,)), ((), ())), preferred_element_type=F32
        )
        if h == 0:
            glift[...] = gl
            pass_on(HID // CHUNK - 1)
        else:
            glift[...] += gl

    for t in range(CAP):
        here = slice(t * 64, t * 64 + 64)
        gn = [glift[here, g * 128 : g * 128 + 128] * gain_row[:, g * 128 : g * 128 + 128] for g in range(CG)]
        n = [normed[g, t].reshape(64, 128) for g in range(CG)]
        m1 = jnp.sum(gn[0] + gn[1] + gn[2], axis=-1, keepdims=True) / C
        m2 = jnp.sum(gn[0] * n[0] + gn[1] * n[1] + gn[2] * n[2], axis=-1, keepdims=True) / C
        for g in range(CG):
            gc = (inv[t] * (gn[g] - m1 - n[g] * m2)).reshape(TILE, TILE, 128)
            gconv[g, t] = gc
            edge_first[g, t] = gc[:3].astype(BF16)
            edge_last[g, t] = gc[TILE - 3 :].astype(BF16)
    to_after = copy_to(after, edge_last, north_g, s_halo.at[0], r_halo.at[0])
    to_before = copy_to(before, edge_first, south_g, s_halo.at[1], r_halo.at[1])
    to_after.start()
    to_before.start()

    emb_pair.wait_recv()
    emb_sum[...] = emb[...] + emb1[...]
    across = copy_to(at(dp, 1 - plane, z), emb_sum, emb2, s_e.at[1], r_e.at[1])
    across.start()

    @pl.loop(0, CG)
    def _(g):
        for j in range(7):

            def tile_taps(t, carry, j=j):
                gc = [gconv[g, t, a] for a in range(TILE)]
                total = list(carry)
                for r in range(14):
                    window = pad[g, t, r, 5 + j : 13 + j, :]
                    for i in range(7):
                        a = r - i
                        if 0 <= a < TILE:
                            total[i] = total[i] + window * gc[a]
                return tuple(total)

            sums = lax.fori_loop(
                0, CAP, tile_taps, tuple(jnp.zeros((8, 128), F32) for _ in range(7))
            )
            for i in range(7):
                kparts[g, i * 7 + j] = sums[i]

    for g in range(CG):
        lanes = slice(g * 128, g * 128 + 128)
        total = jnp.sum(kparts[g], axis=1)
        total = jnp.concatenate([total, jnp.zeros((15, 128), F32)], axis=0)
        for q in range(16):
            kgrads[q, :, lanes] = total[q * 4 : q * 4 + 4].astype(BF16)
    kpair = copy_to(partner, kgrads, kgot1, s1k.at[0], r1k.at[0])
    kpair.start()

    def from_tiles(i):
        return [gconv[g, i] for g in range(CG)]

    def from_edge(ref):
        return lambda i: [ref[g, i].astype(F32) for g in range(CG)]

    @pl.loop(0, CAP)
    def _(t):
        spread(adj, t, pad_g, from_tiles, None, None)

    def kplane(n, arriving=False):
        q, device = plane_device(*PLANE_ORDER[n])
        slot = q if arriving else spot
        return copy_to(device, ksend2.at[q], kgot2.at[slot], s2k.at[n], r2k.at[slot])

    kpair.wait_recv()
    ksend2[...] = (kgrads[...].astype(F32) + kgot1[...].astype(F32)).astype(BF16)
    for n in range(15):
        kplane(n).start()
    kgot2[spot] = ksend2[spot]

    to_after.wait_recv()
    to_before.wait_recv()

    @pl.loop(0, CAP)
    def _(t):
        spread(adj, t, pad_g, None, from_edge(north_g), from_edge(south_g))
        live = live_of(cnt, t)
        for g in range(CG):
            lanes = slice(g * 128, g * 128 + 128)
            rows = conv_tile(pad_g, taps, g, t, True)
            extra = pw[0, t] * cot[:, lanes] / TILE
            for a in range(TILE):
                g_out = live * (up[t, a, :, lanes].astype(F32) + extra)
                out[t, a, :, lanes] = (live * (g_out + rows[a])).astype(BF16)

    out_copy = pltpu.make_async_copy(out, out_hbm, out_sems.at[0])
    out_copy.start()
    down.wait_send()
    upward.wait_send()
    across.wait_recv()
    emb_both = emb_sum[0:1] + emb2[0:1]
    high = emb_both.astype(BF16).astype(F32)
    mine = jnp.where(core == 0, high, emb_both - high)
    for h in range(HID // CHUNK):
        pair_of(h).wait_send()
    emb_pair.wait_send()
    kpair.wait_send()
    to_after.wait_send()
    to_before.wait_send()

    for n in range(15):
        kplane(n, True).wait_recv()
        q, device = plane_device(*PLANE_ORDER[n])
        for hh in range(2):
            copy_to(device, send2.at[0, 0], got2.at[q, hh], s2.at[0, 0], r2.at[q, hh]).wait_recv()

    total = [got2[0, hh].astype(F32) for hh in range(2)]
    tail = kgot2[0].astype(F32)
    for q in range(1, 16):
        total = [total[hh] + got2[q, hh].astype(F32) for hh in range(2)]
        tail = tail + kgot2[q].astype(F32)

    for q in range(16):
        row = q % 8 * 3
        send3[q] = jnp.concatenate([total[q // 8][row : row + 3], tail, mine], axis=0).astype(BF16)

    def ring(k, arriving=False):
        q = wrapped(z + k, 16)
        slot = q if arriving else z
        return copy_to(at(dp, plane, q), send3.at[q], got3.at[slot], s3.at[k], r3.at[slot])

    for k in RING_ORDER:
        ring(k).start()

    got3[z] = send3[z]
    across.wait_send()
    for h in range(HID // CHUNK):

        for k in DP_ORDER:
            plane_of(h, k).wait_send()

        @pl.when(plane != h // 2)
        def _():
            plane_of(h, 0).wait_send()

    for n in range(15):
        kplane(n).wait_send()
    for k in RING_ORDER:
        ring(k, True).wait_recv()

    total = got3[0].astype(F32)
    for q in range(1, 16):
        total = total + got3[q].astype(F32)

    send4[...] = total.astype(BF16)
    half[...] = jnp.broadcast_to(total[7:8], (8, C))

    def last(n, arriving=False):
        q, device = plane_device(*PLANE_ORDER[n])
        slot = q if arriving else spot
        return copy_to(device, send4, got4.at[slot], s4.at[n], r4.at[slot])

    for n in range(15):
        last(n).start()

    swap = copy_to(partner, half, other, s5.at[0], r5.at[0])
    swap.start()
    own_copy = pltpu.make_async_copy(send4, got4.at[spot], out_sems.at[1])
    own_copy.start()

    for k in RING_ORDER:
        ring(k).wait_send()

    swap.wait()
    emb_out[...] = half[...] + other[...]
    emb_copy = pltpu.make_async_copy(emb_out, emb_hbm, out_sems.at[2])
    emb_copy.start()
    out_copy.wait()
    own_copy.wait()
    emb_copy.wait()

    for n in range(15):
        last(n, True).wait_recv()
    for n in range(15):
        last(n).wait_send()


def finish_kernel(out, got4_in, emb_in, emb, tiles, w_grad, k_grad, got4, emb_got, sems):
    plane = lax.axis_index("space") // 32
    loads = [
        pltpu.make_async_copy(got4_in, got4, sems.at[0]),
        pltpu.make_async_copy(emb_in, emb_got, sems.at[1]),
        pltpu.make_async_copy(out, tiles, sems.at[2]),
    ]
    for load in loads:
        load.start()
    loads[0].wait()
    for d in range(8):
        w_grad[d * 3 : d * 3 + 3, :] = got4[d * 2 + plane, 0:3].astype(F32)
    for ij in range(49):
        row = got4[ij // 4, 3 + ij % 4 : 4 + ij % 4].astype(F32)
        k_grad[ij // 7, ij % 7 : ij % 7 + 1, :] = row
    loads[1].wait()
    emb[...] = emb_got[0:1]
    loads[2].wait()


VMEM = pl.BlockSpec(memory_space=pltpu.VMEM)
SMEM = pl.BlockSpec(memory_space=pltpu.SMEM)
HBM = pl.BlockSpec(memory_space=pltpu.HBM)


def vmem(shape, dtype):
    return pltpu.VMEM(shape, dtype)


def per_device(
    tiles_in, upstream, pool_weight, slide_cot, adjacency, counts, kernel, norm_gain, w_in, w_out,
    layer_scale,
):
    own, up = tiles_in[0], upstream[0]
    spaces = lax.axis_size("space")
    struct = jax.ShapeDtypeStruct
    dma = pltpu.SemaphoreType.DMA
    edge = (CG, CAP, 3, TILE, 128)
    halo = (CAP, 3, TILE, C)
    blocks = (CG, CAP, TILE, TILE, 128)
    chunks = HID // CHUNK

    out, got4, emb = pl.pallas_call(
        functools.partial(main_kernel, spaces),
        out_shape=(
            struct((CAP, TILE, TILE, C), BF16),
            struct((16, 8, C), BF16),
            struct((8, C), F32),
        ),
        in_specs=[SMEM] * 3 + [HBM] * 8,
        out_specs=(HBM,) * 3,
        scratch_shapes=[
            vmem((CAP, TILE, TILE, C), BF16),
            vmem((8, C), F32),
            dma((3,)),
            vmem((CAP, TILE, TILE, C), BF16),
            vmem(halo, BF16),
            vmem(halo, BF16),
            vmem((CAP, TILE, TILE, C), BF16),
            vmem((1, C), F32),
            vmem((7, 7, C), F32),
            vmem((C,), F32),
            vmem((C,), F32),
            vmem((C, HID), BF16),
            vmem((HID, C), BF16),
            dma((8,)),
            vmem((CG, CAP, 14, 24, 128), F32),
            vmem((CG, CAP, 14, 24, 128), F32),
            vmem((CG, 49, 8, 128), F32),
            vmem(blocks, F32),
            vmem((CAP, 64, 128), F32),
            vmem((PIX, C), BF16),
            vmem((PIX, C), BF16),
            vmem((PIX, C), F32),
            vmem((PIX, HID), F32),
            vmem((PIX, HID), F32),
            vmem((CHUNK, CHUNK), BF16),
            vmem(blocks, F32),
            vmem((CG, 49, 8, 128), F32),
            vmem((2, chunks, 8, 24, C), BF16),
            vmem((chunks, 8, 24, C), BF16),
            vmem((chunks, 8, 24, C), BF16),
            vmem((16, 2, 24, C), BF16),
            vmem((16, 4, C), BF16),
            vmem((16, 4, C), BF16),
            vmem((16, 4, C), BF16),
            vmem((16, 4, C), BF16),
            vmem((8, C), F32),
            vmem((8, C), F32),
            vmem((8, C), F32),
            vmem((8, C), F32),
            vmem((16, 8, C), BF16),
            vmem((16, 8, C), BF16),
            vmem((8, C), BF16),
            vmem((8, C), F32),
            vmem((8, C), F32),
            vmem(edge, BF16),
            vmem(edge, BF16),
            vmem(edge, BF16),
            vmem(edge, BF16),
            dma((2,)), dma((2,)),
            dma((2,)), dma((2,)),
            dma((chunks,)), dma((chunks,)),
            dma((1,)), dma((1,)),
            dma((chunks, 8)), dma((16, 2)),
            dma((16,)), dma((16,)),
            dma((2,)), dma((2,)),
            dma((16,)), dma((16,)),
            dma((16,)), dma((16,)),
            dma((1,)), dma((1,)),
        ],
        compiler_params=pltpu.CompilerParams(
            collective_id=0, has_side_effects=True, vmem_limit_bytes=VMEM_BYTES
        ),
        name="main",
    )(
        pool_weight, adjacency[0], counts, own, up, slide_cot, kernel, norm_gain, layer_scale, w_in,
        w_out,
    )

    embedding, grad_tiles, w_grad, k_grad = pl.pallas_call(
        finish_kernel,
        out_shape=(
            struct((1, C), F32),
            struct((CAP, TILE, TILE, C), BF16),
            struct((24, C), F32),
            struct((7, 7, C), F32),
        ),
        in_specs=[HBM] * 3,
        out_specs=(VMEM,) * 4,
        scratch_shapes=[vmem((16, 8, C), BF16), vmem((8, C), F32), dma((3,))],
        name="finish",
    )(out, got4, emb)
    return embedding, grad_tiles[None], w_grad, k_grad


def solution(mesh):
    return jax.shard_map(
        per_device,
        mesh=mesh,
        in_specs=(
            P("dp", "space", None, None, None),
            P("dp", "space", None, None, None),
            P("dp", "space"),
            P("dp", None),
            P("dp", "space", None),
            P("dp", "space"),
            P(),
            P(),
            P(),
            P(),
            P(),
        ),
        out_specs=(P("dp", None), P("dp", "space", None, None, None), P("space", None), P()),
        check_vma=False,
    )
```

```python
import contextlib
import functools

import jax
import jax.numpy as jnp
from jax import lax
from jax.experimental import pallas as pl
from jax.experimental.pallas import tpu as pltpu
from jax.sharding import PartitionSpec as P

MESH = pl.DeviceIdType.MESH
F32, BF16 = jnp.float32, jnp.bfloat16
sqrt_half = 0.7071067811865476
inv_root_two_pi = 0.3989422804014327

C, HID, CAP, TILE = 384, 1536, 4, 8
CG = C // 128
PIX = CAP * TILE * TILE
CHUNK = 384
VMEM_BYTES = 60 << 20
SCOPES = False


def scope(name):
    return jax.named_scope(name) if SCOPES else contextlib.nullcontext()


def spread(adj, t, pad, own, north, south):
    def entry(e):
        wanted = adj[t, e]
        return jnp.bitwise_and(jnp.maximum(wanted, 0), CAP - 1), wanted >= 0

    parts = []
    if own is not None:
        parts.append((3, 8, (own, 2), (own, None), (own, 3)))
    if north is not None:
        parts.append((0, 3, (north, 4), (north, 0), (north, 5)))
        parts.append((11, 3, (south, 6), (south, 1), (south, 7)))
    for row, rows, *columns in parts:
        for place, (source, e) in enumerate(columns):
            if e is None:
                groups = source(t)
            else:
                index, valid = entry(e)
                groups = [jnp.where(valid, g, 0.0) for g in source(index)]
            for g in range(CG):
                pad[g, t, row : row + rows, 8 * place : 8 * place + 8, :] = groups[g]


def conv_tile(pad, taps, g, t, flip, rows=range(14), start=None):
    total = list(start) if start is not None else [None] * TILE
    for j in range(7):
        column = [taps[g, 48 - (i * 7 + j) if flip else i * 7 + j] for i in range(7)]
        for r in rows:
            window = pad[g, t, r, 5 + j : 13 + j, :]
            for i in range(7):
                a = r - i
                if 0 <= a < TILE:
                    term = window * column[i]
                    total[a] = term if total[a] is None else total[a] + term
    return total


OWN_ROWS = range(3, 11)
EDGE_ROWS = (0, 1, 2, 11, 12, 13)
RING_ORDER = (8, 7, 9, 6, 10, 5, 11, 4, 12, 3, 13, 2, 14, 1, 15)
PLANE_ORDER = (
    (2, 2), (2, 1), (2, 3), (1, 2), (3, 2), (2, 0), (0, 2), (1, 1), (1, 3), (3, 1), (3, 3), (0, 1),
    (0, 3), (1, 0), (3, 0),
)
DP_ORDER = (4, 5, 3, 2, 6, 7, 1)


def wrapped(value, size):
    return jnp.where(value >= size, value - size, value)


def split_groups(value):
    return [value[..., g * 128 : (g + 1) * 128] for g in range(CG)]


def live_of(cnt, t):
    return jnp.where(t < cnt[0, 0], 1.0, 0.0).astype(F32)


def grad_out_of(up, pw, cot, live, t):
    extra = pw[0, t] * cot[...] / TILE
    return live * (up[t].astype(F32) + extra[None])


def load_taps(ker, taps):
    for ij in range(49):
        row = ker[ij // 7, ij % 7 : ij % 7 + 1, :]
        for g in range(CG):
            taps[g, ij] = jnp.broadcast_to(row[:, g * 128 : (g + 1) * 128], (8, 128))


def copy_to(device, src, dst, send, recv):
    return pltpu.make_async_remote_copy(
        src_ref=src, dst_ref=dst, send_sem=send, recv_sem=recv,
        device_id=device, device_id_type=MESH,
    )


def greet(device):
    pl.semaphore_signal(
        pltpu.get_barrier_semaphore(), inc=1, device_id=device, device_id_type=MESH
    )


def main_kernel(
    spaces,
    pw, adj, cnt,
    own_in, up_in, cot_in, ker_in, gain_in, scale_in, w_in_in, w_out_in,
    out_hbm, got4, emb_hbm,
    out, emb_out, out_sems, own, north, south, up, cot, ker, gain, scale, w_in, w_out, load_sems,
    pad, pad_g, taps, normed, inv, lifted, gmix, glift, slope, gacts, order, gconv, kparts,
    grads, got1, send2, got2, kgrads, kgot1, ksend2, kgot2,
    emb, emb1, emb_sum, emb2, send3, got3, send4, half, other,
    edge_first, edge_last, north_g, south_g,
    heard, s_fore, r_fore, s_halo, r_halo, s1, r1, s1k, r1k, s2, r2, s2k, r2k, s_e, r_e, s3, r3, s4, r4, s5, r5,
):
    dp, space = lax.axis_index("dp"), lax.axis_index("space")
    core = lax.rem(space, 2)
    z = lax.rem(space // 2, 16)
    plane = space // 32
    spot = dp * 2 + plane

    def at(d, p, zz):
        return (d, (p * 16 + zz) * 2 + core)

    px, py = dp // 2, lax.rem(dp, 2) * 2 + plane

    def plane_device(dx, dy):
        x, y = wrapped(px + dx, 4), wrapped(py + dy, 4)
        return x * 4 + y, at(x * 2 + y // 2, lax.rem(y, 2), z)

    partner = (dp, space + 1 - 2 * core)
    before = (dp, lax.rem(space + spaces - 1, spaces))
    after = (dp, lax.rem(space + 1, spaces))

    loads = {}
    sources = dict(
        own=(own_in, own), ker=(ker_in, ker), up=(up_in, up), cot=(cot_in, cot),
        scale=(scale_in, scale), w_out=(w_out_in, w_out), gain=(gain_in, gain), w_in=(w_in_in, w_in),
    )
    for n, (name, (src, dst)) in enumerate(sources.items()):
        loads[name] = pltpu.make_async_copy(src, dst, load_sems.at[n])
        loads[name].start()

    with scope("greet"):
        greet(before)
        greet(after)

        for k in (2, 14, 1, 15):
            greet(at(dp, plane, wrapped(z + k, 16)))
        for d in (2, 1, 3):
            greet(plane_device(d, 0)[1])
            greet(plane_device(0, d)[1])

    with scope("gmix"):
        for name in ("own", "up", "cot", "scale"):
            loads[name].wait()
        scale_row = scale[...].reshape(1, C)
        emb_own = jnp.zeros((1, C), F32)
        for t in range(CAP):
            live = live_of(cnt, t)
            here = slice(t * 64, t * 64 + 64)
            g_out = grad_out_of(up, pw, cot, live, t)
            gmix[here, :] = (g_out * scale_row[None]).astype(BF16).reshape(64, C)
            weight = live * pw[0, t]
            emb_own = emb_own + weight * jnp.sum(
                own[t].astype(F32).reshape(64, C), axis=0, keepdims=True
            )

    with scope("barrier"):
        pl.semaphore_wait(pltpu.get_barrier_semaphore(), 12)

    def tell(device, sem):
        pl.semaphore_signal(sem, inc=1, device_id=device, device_id_type=MESH)

    down = copy_to(after, own.at[:, TILE - 3 :], north, s_fore.at[0], r_fore.at[0])
    upward = copy_to(before, own.at[:, :3], south, s_fore.at[1], r_fore.at[1])
    down.start()
    upward.start()
    for d in (2, 1, 3):
        tell(plane_device(d, 0)[1], heard.at[0])
    for k in (2, 14):
        tell(at(dp, plane, wrapped(z + k, 16)), heard.at[1])

    def groups_of(ref):
        return lambda i: split_groups(ref[i].astype(F32))

    with scope("under_halo"):
        loads["ker"].wait()
        load_taps(ker, taps)

        @pl.loop(0, CAP)
        def _(t):
            spread(adj, t, pad, groups_of(own), None, None)

        d = lax.broadcasted_iota(jnp.int32, (8, CHUNK), 1)
        d_core = jnp.where(d >= 192, 1, 0)
        d = d - 192 * d_core
        d_dp = jnp.zeros_like(d)
        for m in range(1, 8):
            d_dp = d_dp + jnp.where(d >= 24 * m, 1, 0)
        d = d - 24 * d_dp
        d_z = jnp.zeros_like(d)
        for m in range(1, 8):
            d_z = d_z + jnp.where(d >= 3 * m, 1, 0)
        d = d - 3 * d_z
        source = d_z * 48 + d_core * 24 + d_dp * 3 + d
        rows = lax.broadcasted_iota(jnp.int32, (CHUNK, CHUNK), 0)
        order[...] = jnp.where(rows == source[0:1], 1.0, 0.0).astype(BF16)
        loads["w_out"].wait()

        @pl.loop(0, CAP)
        def _(t):
            @pl.loop(0, CG)
            def _(g):
                rows = conv_tile(pad, taps, g, t, False, OWN_ROWS)
                for a in range(TILE):
                    normed[g, t, a] = rows[a]

        for h in range(HID // CHUNK):
            here = slice(h * CHUNK, (h + 1) * CHUNK)
            gacts[:, here] = lax.dot_general(
                gmix[...], w_out[here, :], (((1,), (1,)), ((), ())), preferred_element_type=F32
            )

    with scope("halo_wait"):
        down.wait_recv()
        upward.wait_recv()

    with scope("spread"):

        @pl.loop(0, CAP)
        def _(t):
            spread(adj, t, pad, None, groups_of(north), groups_of(south))

    with scope("conv"):

        @pl.loop(0, CAP)
        def _(t):
            @pl.loop(0, CG)
            def _(g):
                start = [normed[g, t, a] for a in range(TILE)]
                rows = conv_tile(pad, taps, g, t, False, EDGE_ROWS, start)
                for a in range(TILE):
                    normed[g, t, a] = rows[a]

    pl.semaphore_wait(heard.at[0], 3)
    pl.semaphore_wait(heard.at[1], 2)
    for k in (4, 12):
        tell(at(dp, plane, wrapped(z + k, 16)), heard.at[2])

    with scope("norm"):
        loads["gain"].wait()
        gain_row = gain[...].reshape(1, C)
        for t in range(CAP):
            x = [normed[g, t].reshape(64, 128) for g in range(CG)]
            mean = jnp.sum(x[0] + x[1] + x[2], axis=-1, keepdims=True) / C
            x = [v - mean for v in x]
            var = jnp.sum(x[0] * x[0] + x[1] * x[1] + x[2] * x[2], axis=-1, keepdims=True) / C
            istd = jnp.broadcast_to(lax.rsqrt(var + 1e-06), (64, 128))
            inv[t] = istd
            here = slice(t * 64, t * 64 + 64)
            for g in range(CG):
                lanes = slice(g * 128, g * 128 + 128)
                n = x[g] * istd
                normed[g, t] = n.reshape(TILE, TILE, 128)
                lifted[here, lanes] = (n * gain_row[:, lanes]).astype(BF16)
        loads["w_in"].wait()

    def pair_of(h):
        return copy_to(partner, grads.at[1 - core, h], got1.at[h], s1.at[h], r1.at[h])

    def plane_of(h, k):
        to = wrapped(dp + k, 8)
        return copy_to(
            at(to, h // 2, z), send2.at[h, to], got2.at[spot, h % 2], s2.at[h, k],
            r2.at[spot, h % 2],
        )

    def pass_on(h):
        pair_of(h).wait_recv()
        send2[h] = (grads[core, h].astype(F32) + got1[h].astype(F32)).astype(BF16)

        for k in DP_ORDER:
            plane_of(h, k).start()

        @pl.when(plane == h // 2)
        def _():
            got2[spot, h % 2] = send2[h, dp]

        @pl.when(plane != h // 2)
        def _():
            plane_of(h, 0).start()

    mixed = jnp.zeros((8, C), F32)
    for h in range(HID // CHUNK):
        here = slice(h * CHUNK, (h + 1) * CHUNK)
        pre = jnp.dot(lifted[...], w_in[:, here], preferred_element_type=F32)
        cdf = 0.5 * (1.0 + lax.erf(pre * sqrt_half))
        act = (pre * cdf).astype(BF16)
        density = jnp.exp(-0.5 * pre * pre) * inv_root_two_pi
        slope[:, here] = cdf + pre * density
        sent = jnp.dot(act, order[...], preferred_element_type=F32).astype(BF16)
        gw = lax.dot_general(
            sent, gmix[...], (((0,), (0,)), ((), ())), preferred_element_type=F32
        ).astype(BF16)
        for c in range(2):
            for m in range(8):
                grads[c, h, m] = gw[(c * 8 + m) * 24 : (c * 8 + m) * 24 + 24]
        pair_of(h).start()
        pooled = jnp.zeros((1, CHUNK), F32)
        for t in range(CAP):
            weight = live_of(cnt, t) * pw[0, t]
            pooled = pooled + weight * jnp.sum(
                act[t * 64 : t * 64 + 64].astype(F32), axis=0, keepdims=True
            )
        high = pooled.astype(BF16)
        rest = pooled - high.astype(F32)
        middle = rest.astype(BF16)
        low = (rest - middle.astype(F32)).astype(BF16)
        three = jnp.concatenate([high, middle, low, jnp.zeros((5, CHUNK), BF16)], axis=0)
        mixed = mixed + jnp.dot(three, w_out[here, :], preferred_element_type=F32)
        if h > 0:
            pass_on(h - 1)
    mix = jnp.sum(mixed, axis=0, keepdims=True)
    emb[...] = jnp.broadcast_to((emb_own + scale_row * mix) / TILE, (8, C))
    emb_pair = copy_to(partner, emb, emb1, s_e.at[0], r_e.at[0])
    emb_pair.start()

    for h in range(HID // CHUNK):
        here = slice(h * CHUNK, (h + 1) * CHUNK)
        gpre = (gacts[:, here] * slope[:, here]).astype(BF16)
        gl = lax.dot_general(
            gpre, w_in[:, here], (((1,), (1,)), ((), ())), preferred_element_type=F32
        )
        if h == 0:
            glift[...] = gl
            pass_on(HID // CHUNK - 1)
        else:
            glift[...] += gl

    for t in range(CAP):
        here = slice(t * 64, t * 64 + 64)
        gn = [glift[here, g * 128 : g * 128 + 128] * gain_row[:, g * 128 : g * 128 + 128] for g in range(CG)]
        n = [normed[g, t].reshape(64, 128) for g in range(CG)]
        m1 = jnp.sum(gn[0] + gn[1] + gn[2], axis=-1, keepdims=True) / C
        m2 = jnp.sum(gn[0] * n[0] + gn[1] * n[1] + gn[2] * n[2], axis=-1, keepdims=True) / C
        for g in range(CG):
            gc = (inv[t] * (gn[g] - m1 - n[g] * m2)).reshape(TILE, TILE, 128)
            gconv[g, t] = gc
            edge_first[g, t] = gc[:3].astype(BF16)
            edge_last[g, t] = gc[TILE - 3 :].astype(BF16)
    to_after = copy_to(after, edge_last, north_g, s_halo.at[0], r_halo.at[0])
    to_before = copy_to(before, edge_first, south_g, s_halo.at[1], r_halo.at[1])
    to_after.start()
    to_before.start()

    emb_pair.wait_recv()
    emb_sum[...] = emb[...] + emb1[...]
    across = copy_to(at(dp, 1 - plane, z), emb_sum, emb2, s_e.at[1], r_e.at[1])
    across.start()

    @pl.loop(0, CG)
    def _(g):
        for j in range(7):

            def tile_taps(t, carry, j=j):
                gc = [gconv[g, t, a] for a in range(TILE)]
                total = list(carry)
                for r in range(14):
                    window = pad[g, t, r, 5 + j : 13 + j, :]
                    for i in range(7):
                        a = r - i
                        if 0 <= a < TILE:
                            total[i] = total[i] + window * gc[a]
                return tuple(total)

            sums = lax.fori_loop(
                0, CAP, tile_taps, tuple(jnp.zeros((8, 128), F32) for _ in range(7))
            )
            for i in range(7):
                kparts[g, i * 7 + j] = sums[i]

    for g in range(CG):
        lanes = slice(g * 128, g * 128 + 128)
        total = jnp.sum(kparts[g], axis=1)
        total = jnp.concatenate([total, jnp.zeros((15, 128), F32)], axis=0)
        for q in range(16):
            kgrads[q, :, lanes] = total[q * 4 : q * 4 + 4].astype(BF16)
    kpair = copy_to(partner, kgrads, kgot1, s1k.at[0], r1k.at[0])
    kpair.start()

    def from_tiles(i):
        return [gconv[g, i] for g in range(CG)]

    def from_edge(ref):
        return lambda i: [ref[g, i].astype(F32) for g in range(CG)]

    @pl.loop(0, CAP)
    def _(t):
        spread(adj, t, pad_g, from_tiles, None, None)

    def kplane(n, arriving=False):
        q, device = plane_device(*PLANE_ORDER[n])
        slot = q if arriving else spot
        return copy_to(device, ksend2.at[q], kgot2.at[slot], s2k.at[n], r2k.at[slot])

    kpair.wait_recv()
    ksend2[...] = (kgrads[...].astype(F32) + kgot1[...].astype(F32)).astype(BF16)
    for n in range(15):
        kplane(n).start()
    kgot2[spot] = ksend2[spot]

    to_after.wait_recv()
    to_before.wait_recv()

    @pl.loop(0, CAP)
    def _(t):
        spread(adj, t, pad_g, None, from_edge(north_g), from_edge(south_g))
        live = live_of(cnt, t)
        for g in range(CG):
            lanes = slice(g * 128, g * 128 + 128)
            rows = conv_tile(pad_g, taps, g, t, True)
            extra = pw[0, t] * cot[:, lanes] / TILE
            for a in range(TILE):
                g_out = live * (up[t, a, :, lanes].astype(F32) + extra)
                out[t, a, :, lanes] = (live * (g_out + rows[a])).astype(BF16)

    out_copy = pltpu.make_async_copy(out, out_hbm, out_sems.at[0])
    out_copy.start()
    down.wait_send()
    upward.wait_send()
    across.wait_recv()
    emb_both = emb_sum[0:1] + emb2[0:1]
    high = emb_both.astype(BF16).astype(F32)
    mine = jnp.where(core == 0, high, emb_both - high)
    for h in range(HID // CHUNK):
        pair_of(h).wait_send()
    emb_pair.wait_send()
    kpair.wait_send()
    to_after.wait_send()
    to_before.wait_send()

    for n in range(15):
        kplane(n, True).wait_recv()
        q, device = plane_device(*PLANE_ORDER[n])
        for hh in range(2):
            copy_to(device, send2.at[0, 0], got2.at[q, hh], s2.at[0, 0], r2.at[q, hh]).wait_recv()

    total = [got2[0, hh].astype(F32) for hh in range(2)]
    tail = kgot2[0].astype(F32)
    for q in range(1, 16):
        total = [total[hh] + got2[q, hh].astype(F32) for hh in range(2)]
        tail = tail + kgot2[q].astype(F32)

    pl.semaphore_wait(heard.at[2], 2)

    for q in range(16):
        row = q % 8 * 3
        send3[q] = jnp.concatenate([total[q // 8][row : row + 3], tail, mine], axis=0).astype(BF16)

    def ring(k, arriving=False):
        q = wrapped(z + k, 16)
        slot = q if arriving else z
        return copy_to(at(dp, plane, q), send3.at[q], got3.at[slot], s3.at[k], r3.at[slot])

    for k in RING_ORDER:
        ring(k).start()

    got3[z] = send3[z]
    across.wait_send()
    for h in range(HID // CHUNK):

        for k in DP_ORDER:
            plane_of(h, k).wait_send()

        @pl.when(plane != h // 2)
        def _():
            plane_of(h, 0).wait_send()

    for n in range(15):
        kplane(n).wait_send()
    for k in RING_ORDER:
        ring(k, True).wait_recv()

    total = got3[0].astype(F32)
    for q in range(1, 16):
        total = total + got3[q].astype(F32)

    send4[...] = total.astype(BF16)
    half[...] = jnp.broadcast_to(total[7:8], (8, C))

    def last(n, arriving=False):
        q, device = plane_device(*PLANE_ORDER[n])
        slot = q if arriving else spot
        return copy_to(device, send4, got4.at[slot], s4.at[n], r4.at[slot])

    for n in range(15):
        last(n).start()

    swap = copy_to(partner, half, other, s5.at[0], r5.at[0])
    swap.start()
    own_copy = pltpu.make_async_copy(send4, got4.at[spot], out_sems.at[1])
    own_copy.start()

    for k in RING_ORDER:
        ring(k).wait_send()

    swap.wait()
    emb_out[...] = half[...] + other[...]
    emb_copy = pltpu.make_async_copy(emb_out, emb_hbm, out_sems.at[2])
    emb_copy.start()
    out_copy.wait()
    own_copy.wait()
    emb_copy.wait()

    for n in range(15):
        last(n, True).wait_recv()
    for n in range(15):
        last(n).wait_send()


def finish_kernel(out, got4_in, emb_in, emb, tiles, w_grad, k_grad, got4, emb_got, sems):
    plane = lax.axis_index("space") // 32
    loads = [
        pltpu.make_async_copy(got4_in, got4, sems.at[0]),
        pltpu.make_async_copy(emb_in, emb_got, sems.at[1]),
        pltpu.make_async_copy(out, tiles, sems.at[2]),
    ]
    for load in loads:
        load.start()
    loads[0].wait()
    for d in range(8):
        w_grad[d * 3 : d * 3 + 3, :] = got4[d * 2 + plane, 0:3].astype(F32)
    for ij in range(49):
        row = got4[ij // 4, 3 + ij % 4 : 4 + ij % 4].astype(F32)
        k_grad[ij // 7, ij % 7 : ij % 7 + 1, :] = row
    loads[1].wait()
    emb[...] = emb_got[0:1]
    loads[2].wait()


VMEM = pl.BlockSpec(memory_space=pltpu.VMEM)
SMEM = pl.BlockSpec(memory_space=pltpu.SMEM)
HBM = pl.BlockSpec(memory_space=pltpu.HBM)


def vmem(shape, dtype):
    return pltpu.VMEM(shape, dtype)


def per_device(
    tiles_in, upstream, pool_weight, slide_cot, adjacency, counts, kernel, norm_gain, w_in, w_out,
    layer_scale,
):
    own, up = tiles_in[0], upstream[0]
    spaces = lax.axis_size("space")
    struct = jax.ShapeDtypeStruct
    dma = pltpu.SemaphoreType.DMA
    edge = (CG, CAP, 3, TILE, 128)
    halo = (CAP, 3, TILE, C)
    blocks = (CG, CAP, TILE, TILE, 128)
    chunks = HID // CHUNK

    out, got4, emb = pl.pallas_call(
        functools.partial(main_kernel, spaces),
        out_shape=(
            struct((CAP, TILE, TILE, C), BF16),
            struct((16, 8, C), BF16),
            struct((8, C), F32),
        ),
        in_specs=[SMEM] * 3 + [HBM] * 8,
        out_specs=(HBM,) * 3,
        scratch_shapes=[
            vmem((CAP, TILE, TILE, C), BF16),
            vmem((8, C), F32),
            dma((3,)),
            vmem((CAP, TILE, TILE, C), BF16),
            vmem(halo, BF16),
            vmem(halo, BF16),
            vmem((CAP, TILE, TILE, C), BF16),
            vmem((1, C), F32),
            vmem((7, 7, C), F32),
            vmem((C,), F32),
            vmem((C,), F32),
            vmem((C, HID), BF16),
            vmem((HID, C), BF16),
            dma((8,)),
            vmem((CG, CAP, 14, 24, 128), F32),
            vmem((CG, CAP, 14, 24, 128), F32),
            vmem((CG, 49, 8, 128), F32),
            vmem(blocks, F32),
            vmem((CAP, 64, 128), F32),
            vmem((PIX, C), BF16),
            vmem((PIX, C), BF16),
            vmem((PIX, C), F32),
            vmem((PIX, HID), F32),
            vmem((PIX, HID), F32),
            vmem((CHUNK, CHUNK), BF16),
            vmem(blocks, F32),
            vmem((CG, 49, 8, 128), F32),
            vmem((2, chunks, 8, 24, C), BF16),
            vmem((chunks, 8, 24, C), BF16),
            vmem((chunks, 8, 24, C), BF16),
            vmem((16, 2, 24, C), BF16),
            vmem((16, 4, C), BF16),
            vmem((16, 4, C), BF16),
            vmem((16, 4, C), BF16),
            vmem((16, 4, C), BF16),
            vmem((8, C), F32),
            vmem((8, C), F32),
            vmem((8, C), F32),
            vmem((8, C), F32),
            vmem((16, 8, C), BF16),
            vmem((16, 8, C), BF16),
            vmem((8, C), BF16),
            vmem((8, C), F32),
            vmem((8, C), F32),
            vmem(edge, BF16),
            vmem(edge, BF16),
            vmem(edge, BF16),
            vmem(edge, BF16),
            pltpu.SemaphoreType.REGULAR((3,)),
            dma((2,)), dma((2,)),
            dma((2,)), dma((2,)),
            dma((chunks,)), dma((chunks,)),
            dma((1,)), dma((1,)),
            dma((chunks, 8)), dma((16, 2)),
            dma((16,)), dma((16,)),
            dma((2,)), dma((2,)),
            dma((16,)), dma((16,)),
            dma((16,)), dma((16,)),
            dma((1,)), dma((1,)),
        ],
        compiler_params=pltpu.CompilerParams(
            collective_id=0, has_side_effects=True, vmem_limit_bytes=VMEM_BYTES
        ),
        name="main",
    )(
        pool_weight, adjacency[0], counts, own, up, slide_cot, kernel, norm_gain, layer_scale, w_in,
        w_out,
    )

    embedding, grad_tiles, w_grad, k_grad = pl.pallas_call(
        finish_kernel,
        out_shape=(
            struct((1, C), F32),
            struct((CAP, TILE, TILE, C), BF16),
            struct((24, C), F32),
            struct((7, 7, C), F32),
        ),
        in_specs=[HBM] * 3,
        out_specs=(VMEM,) * 4,
        scratch_shapes=[vmem((16, 8, C), BF16), vmem((8, C), F32), dma((3,))],
        name="finish",
    )(out, got4, emb)
    return embedding, grad_tiles[None], w_grad, k_grad


def solution(mesh):
    return jax.shard_map(
        per_device,
        mesh=mesh,
        in_specs=(
            P("dp", "space", None, None, None),
            P("dp", "space", None, None, None),
            P("dp", "space"),
            P("dp", None),
            P("dp", "space", None),
            P("dp", "space"),
            P(),
            P(),
            P(),
            P(),
            P(),
        ),
        out_specs=(P("dp", None), P("dp", "space", None, None, None), P("space", None), P()),
        check_vma=False,
    )
```

```python
import contextlib
import functools

import jax
import jax.numpy as jnp
from jax import lax
from jax.experimental import pallas as pl
from jax.experimental.pallas import tpu as pltpu
from jax.sharding import PartitionSpec as P

MESH = pl.DeviceIdType.MESH
F32, BF16 = jnp.float32, jnp.bfloat16
sqrt_half = 0.7071067811865476
inv_root_two_pi = 0.3989422804014327

C, HID, CAP, TILE = 384, 1536, 4, 8
CG = C // 128
PIX = CAP * TILE * TILE
CHUNK = 384
VMEM_BYTES = 60 << 20
SCOPES = False


def scope(name):
    return jax.named_scope(name) if SCOPES else contextlib.nullcontext()


def spread(adj, t, pad, own, north, south):
    def entry(e):
        wanted = adj[t, e]
        return jnp.bitwise_and(jnp.maximum(wanted, 0), CAP - 1), wanted >= 0

    parts = []
    if own is not None:
        parts.append((3, 8, (own, 2), (own, None), (own, 3)))
    if north is not None:
        parts.append((0, 3, (north, 4), (north, 0), (north, 5)))
        parts.append((11, 3, (south, 6), (south, 1), (south, 7)))
    for row, rows, *columns in parts:
        for place, (source, e) in enumerate(columns):
            if e is None:
                groups = source(t)
            else:
                index, valid = entry(e)
                groups = [jnp.where(valid, g, 0.0) for g in source(index)]
            for g in range(CG):
                pad[g, t, row : row + rows, 8 * place : 8 * place + 8, :] = groups[g]


def conv_tile(pad, taps, g, t, flip, rows=range(14), start=None):
    total = list(start) if start is not None else [None] * TILE
    for j in range(7):
        column = [taps[g, 48 - (i * 7 + j) if flip else i * 7 + j] for i in range(7)]
        for r in rows:
            window = pad[g, t, r, 5 + j : 13 + j, :]
            for i in range(7):
                a = r - i
                if 0 <= a < TILE:
                    term = window * column[i]
                    total[a] = term if total[a] is None else total[a] + term
    return total


OWN_ROWS = range(3, 11)
EDGE_ROWS = (0, 1, 2, 11, 12, 13)
RING_ORDER = (8, 7, 9, 6, 10, 5, 11, 4, 12, 3, 13, 2, 14, 1, 15)
PLANE_ORDER = (
    (2, 2), (2, 1), (2, 3), (1, 2), (3, 2), (2, 0), (0, 2), (1, 1), (1, 3), (3, 1), (3, 3), (0, 1),
    (0, 3), (1, 0), (3, 0),
)
DP_ORDER = (4, 5, 3, 2, 6, 7, 1)


def wrapped(value, size):
    return jnp.where(value >= size, value - size, value)


def split_groups(value):
    return [value[..., g * 128 : (g + 1) * 128] for g in range(CG)]


def live_of(cnt, t):
    return jnp.where(t < cnt[0, 0], 1.0, 0.0).astype(F32)


def grad_out_of(up, pw, cot, live, t):
    extra = pw[0, t] * cot[...] / TILE
    return live * (up[t].astype(F32) + extra[None])


def load_taps(ker, taps):
    for ij in range(49):
        row = ker[ij // 7, ij % 7 : ij % 7 + 1, :]
        for g in range(CG):
            taps[g, ij] = jnp.broadcast_to(row[:, g * 128 : (g + 1) * 128], (8, 128))


def copy_to(device, src, dst, send, recv):
    return pltpu.make_async_remote_copy(
        src_ref=src, dst_ref=dst, send_sem=send, recv_sem=recv,
        device_id=device, device_id_type=MESH,
    )


def greet(device):
    pl.semaphore_signal(
        pltpu.get_barrier_semaphore(), inc=1, device_id=device, device_id_type=MESH
    )


def main_kernel(
    spaces,
    pw, adj, cnt,
    own_in, up_in, cot_in, ker_in, gain_in, scale_in, w_in_in, w_out_in,
    out_hbm, got4, emb_hbm,
    out, emb_out, out_sems, own, north, south, up, cot, ker, gain, scale, w_in, w_out, load_sems,
    pad, pad_g, taps, normed, inv, lifted, gmix, glift, slope, gacts, order, gconv, kparts,
    grads, got1, send2, got2, kgrads, kgot1, ksend2, kgot2,
    emb, emb1, emb_sum, emb2, send3, got3, send4, half, other,
    edge_first, edge_last, north_g, south_g,
    heard, s_fore, r_fore, s_halo, r_halo, s1, r1, s1k, r1k, s2, r2, s2k, r2k, s_e, r_e, s3, r3, s4, r4, s5, r5,
):
    dp, space = lax.axis_index("dp"), lax.axis_index("space")
    core = lax.rem(space, 2)
    z = lax.rem(space // 2, 16)
    plane = space // 32
    spot = dp * 2 + plane

    def at(d, p, zz):
        return (d, (p * 16 + zz) * 2 + core)

    px, py = dp // 2, lax.rem(dp, 2) * 2 + plane

    def plane_device(dx, dy):
        x, y = wrapped(px + dx, 4), wrapped(py + dy, 4)
        return x * 4 + y, at(x * 2 + y // 2, lax.rem(y, 2), z)

    partner = (dp, space + 1 - 2 * core)
    before = (dp, lax.rem(space + spaces - 1, spaces))
    after = (dp, lax.rem(space + 1, spaces))

    loads = {}
    sources = dict(
        own=(own_in, own), ker=(ker_in, ker), up=(up_in, up), cot=(cot_in, cot),
        scale=(scale_in, scale), w_out=(w_out_in, w_out), gain=(gain_in, gain), w_in=(w_in_in, w_in),
    )
    for n, (name, (src, dst)) in enumerate(sources.items()):
        loads[name] = pltpu.make_async_copy(src, dst, load_sems.at[n])
        loads[name].start()

    with scope("greet"):
        greet(before)
        greet(after)

        for k in (2, 14, 1, 15):
            greet(at(dp, plane, wrapped(z + k, 16)))
        for d in (2, 1, 3):
            greet(plane_device(d, 0)[1])
            greet(plane_device(0, d)[1])

    with scope("barrier"):
        pl.semaphore_wait(pltpu.get_barrier_semaphore(), 12)

    def tell(device, sem):
        pl.semaphore_signal(sem, inc=1, device_id=device, device_id_type=MESH)

    loads["own"].wait()
    down = copy_to(after, own.at[:, TILE - 3 :], north, s_fore.at[0], r_fore.at[0])
    upward = copy_to(before, own.at[:, :3], south, s_fore.at[1], r_fore.at[1])
    down.start()
    upward.start()
    for d in (2, 1, 3):
        tell(plane_device(d, 0)[1], heard.at[0])
    for k in (2, 14):
        tell(at(dp, plane, wrapped(z + k, 16)), heard.at[1])

    with scope("gmix"):
        for name in ("up", "cot", "scale"):
            loads[name].wait()
        scale_row = scale[...].reshape(1, C)
        emb_own = jnp.zeros((1, C), F32)
        for t in range(CAP):
            live = live_of(cnt, t)
            here = slice(t * 64, t * 64 + 64)
            g_out = grad_out_of(up, pw, cot, live, t)
            gmix[here, :] = (g_out * scale_row[None]).astype(BF16).reshape(64, C)
            weight = live * pw[0, t]
            emb_own = emb_own + weight * jnp.sum(
                own[t].astype(F32).reshape(64, C), axis=0, keepdims=True
            )

    def groups_of(ref):
        return lambda i: split_groups(ref[i].astype(F32))

    with scope("under_halo"):
        loads["ker"].wait()
        load_taps(ker, taps)

        @pl.loop(0, CAP)
        def _(t):
            spread(adj, t, pad, groups_of(own), None, None)

        d = lax.broadcasted_iota(jnp.int32, (8, CHUNK), 1)
        d_core = jnp.where(d >= 192, 1, 0)
        d = d - 192 * d_core
        d_dp = jnp.zeros_like(d)
        for m in range(1, 8):
            d_dp = d_dp + jnp.where(d >= 24 * m, 1, 0)
        d = d - 24 * d_dp
        d_z = jnp.zeros_like(d)
        for m in range(1, 8):
            d_z = d_z + jnp.where(d >= 3 * m, 1, 0)
        d = d - 3 * d_z
        source = d_z * 48 + d_core * 24 + d_dp * 3 + d
        rows = lax.broadcasted_iota(jnp.int32, (CHUNK, CHUNK), 0)
        order[...] = jnp.where(rows == source[0:1], 1.0, 0.0).astype(BF16)
        loads["w_out"].wait()

        @pl.loop(0, CAP)
        def _(t):
            @pl.loop(0, CG)
            def _(g):
                rows = conv_tile(pad, taps, g, t, False, OWN_ROWS)
                for a in range(TILE):
                    normed[g, t, a] = rows[a]

        for h in range(HID // CHUNK):
            here = slice(h * CHUNK, (h + 1) * CHUNK)
            gacts[:, here] = lax.dot_general(
                gmix[...], w_out[here, :], (((1,), (1,)), ((), ())), preferred_element_type=F32
            )

    with scope("halo_wait"):
        down.wait_recv()
        upward.wait_recv()

    with scope("spread"):

        @pl.loop(0, CAP)
        def _(t):
            spread(adj, t, pad, None, groups_of(north), groups_of(south))

    with scope("conv"):

        @pl.loop(0, CAP)
        def _(t):
            @pl.loop(0, CG)
            def _(g):
                start = [normed[g, t, a] for a in range(TILE)]
                rows = conv_tile(pad, taps, g, t, False, EDGE_ROWS, start)
                for a in range(TILE):
                    normed[g, t, a] = rows[a]

    pl.semaphore_wait(heard.at[0], 3)
    pl.semaphore_wait(heard.at[1], 2)
    for k in (4, 12):
        tell(at(dp, plane, wrapped(z + k, 16)), heard.at[2])

    with scope("norm"):
        loads["gain"].wait()
        gain_row = gain[...].reshape(1, C)
        for t in range(CAP):
            x = [normed[g, t].reshape(64, 128) for g in range(CG)]
            mean = jnp.sum(x[0] + x[1] + x[2], axis=-1, keepdims=True) / C
            x = [v - mean for v in x]
            var = jnp.sum(x[0] * x[0] + x[1] * x[1] + x[2] * x[2], axis=-1, keepdims=True) / C
            istd = jnp.broadcast_to(lax.rsqrt(var + 1e-06), (64, 128))
            inv[t] = istd
            here = slice(t * 64, t * 64 + 64)
            for g in range(CG):
                lanes = slice(g * 128, g * 128 + 128)
                n = x[g] * istd
                normed[g, t] = n.reshape(TILE, TILE, 128)
                lifted[here, lanes] = (n * gain_row[:, lanes]).astype(BF16)
        loads["w_in"].wait()

    def pair_of(h):
        return copy_to(partner, grads.at[1 - core, h], got1.at[h], s1.at[h], r1.at[h])

    def plane_of(h, k):
        to = wrapped(dp + k, 8)
        return copy_to(
            at(to, h // 2, z), send2.at[h, to], got2.at[spot, h % 2], s2.at[h, k],
            r2.at[spot, h % 2],
        )

    def pass_on(h):
        pair_of(h).wait_recv()
        send2[h] = (grads[core, h].astype(F32) + got1[h].astype(F32)).astype(BF16)

        for k in DP_ORDER:
            plane_of(h, k).start()

        @pl.when(plane == h // 2)
        def _():
            got2[spot, h % 2] = send2[h, dp]

        @pl.when(plane != h // 2)
        def _():
            plane_of(h, 0).start()

    mixed = jnp.zeros((8, C), F32)
    for h in range(HID // CHUNK):
        here = slice(h * CHUNK, (h + 1) * CHUNK)
        pre = jnp.dot(lifted[...], w_in[:, here], preferred_element_type=F32)
        cdf = 0.5 * (1.0 + lax.erf(pre * sqrt_half))
        act = (pre * cdf).astype(BF16)
        density = jnp.exp(-0.5 * pre * pre) * inv_root_two_pi
        slope[:, here] = cdf + pre * density
        sent = jnp.dot(act, order[...], preferred_element_type=F32).astype(BF16)
        gw = lax.dot_general(
            sent, gmix[...], (((0,), (0,)), ((), ())), preferred_element_type=F32
        ).astype(BF16)
        for c in range(2):
            for m in range(8):
                grads[c, h, m] = gw[(c * 8 + m) * 24 : (c * 8 + m) * 24 + 24]
        pair_of(h).start()
        pooled = jnp.zeros((1, CHUNK), F32)
        for t in range(CAP):
            weight = live_of(cnt, t) * pw[0, t]
            pooled = pooled + weight * jnp.sum(
                act[t * 64 : t * 64 + 64].astype(F32), axis=0, keepdims=True
            )
        high = pooled.astype(BF16)
        rest = pooled - high.astype(F32)
        middle = rest.astype(BF16)
        low = (rest - middle.astype(F32)).astype(BF16)
        three = jnp.concatenate([high, middle, low, jnp.zeros((5, CHUNK), BF16)], axis=0)
        mixed = mixed + jnp.dot(three, w_out[here, :], preferred_element_type=F32)
        if h > 0:
            pass_on(h - 1)
    mix = jnp.sum(mixed, axis=0, keepdims=True)
    emb[...] = jnp.broadcast_to((emb_own + scale_row * mix) / TILE, (8, C))
    emb_pair = copy_to(partner, emb, emb1, s_e.at[0], r_e.at[0])
    emb_pair.start()

    for h in range(HID // CHUNK):
        here = slice(h * CHUNK, (h + 1) * CHUNK)
        gpre = (gacts[:, here] * slope[:, here]).astype(BF16)
        gl = lax.dot_general(
            gpre, w_in[:, here], (((1,), (1,)), ((), ())), preferred_element_type=F32
        )
        if h == 0:
            glift[...] = gl
            pass_on(HID // CHUNK - 1)
        else:
            glift[...] += gl

    for t in range(CAP):
        here = slice(t * 64, t * 64 + 64)
        gn = [glift[here, g * 128 : g * 128 + 128] * gain_row[:, g * 128 : g * 128 + 128] for g in range(CG)]
        n = [normed[g, t].reshape(64, 128) for g in range(CG)]
        m1 = jnp.sum(gn[0] + gn[1] + gn[2], axis=-1, keepdims=True) / C
        m2 = jnp.sum(gn[0] * n[0] + gn[1] * n[1] + gn[2] * n[2], axis=-1, keepdims=True) / C
        for g in range(CG):
            gc = (inv[t] * (gn[g] - m1 - n[g] * m2)).reshape(TILE, TILE, 128)
            gconv[g, t] = gc
            edge_first[g, t] = gc[:3].astype(BF16)
            edge_last[g, t] = gc[TILE - 3 :].astype(BF16)
    to_after = copy_to(after, edge_last, north_g, s_halo.at[0], r_halo.at[0])
    to_before = copy_to(before, edge_first, south_g, s_halo.at[1], r_halo.at[1])
    to_after.start()
    to_before.start()

    emb_pair.wait_recv()
    emb_sum[...] = emb[...] + emb1[...]
    across = copy_to(at(dp, 1 - plane, z), emb_sum, emb2, s_e.at[1], r_e.at[1])
    across.start()

    @pl.loop(0, CG)
    def _(g):
        for j in range(7):

            def tile_taps(t, carry, j=j):
                gc = [gconv[g, t, a] for a in range(TILE)]
                total = list(carry)
                for r in range(14):
                    window = pad[g, t, r, 5 + j : 13 + j, :]
                    for i in range(7):
                        a = r - i
                        if 0 <= a < TILE:
                            total[i] = total[i] + window * gc[a]
                return tuple(total)

            sums = lax.fori_loop(
                0, CAP, tile_taps, tuple(jnp.zeros((8, 128), F32) for _ in range(7))
            )
            for i in range(7):
                kparts[g, i * 7 + j] = sums[i]

    for g in range(CG):
        lanes = slice(g * 128, g * 128 + 128)
        total = jnp.sum(kparts[g], axis=1)
        total = jnp.concatenate([total, jnp.zeros((15, 128), F32)], axis=0)
        for q in range(16):
            kgrads[q, :, lanes] = total[q * 4 : q * 4 + 4].astype(BF16)
    kpair = copy_to(partner, kgrads, kgot1, s1k.at[0], r1k.at[0])
    kpair.start()

    def from_tiles(i):
        return [gconv[g, i] for g in range(CG)]

    def from_edge(ref):
        return lambda i: [ref[g, i].astype(F32) for g in range(CG)]

    @pl.loop(0, CAP)
    def _(t):
        spread(adj, t, pad_g, from_tiles, None, None)

    def kplane(n, arriving=False):
        q, device = plane_device(*PLANE_ORDER[n])
        slot = q if arriving else spot
        return copy_to(device, ksend2.at[q], kgot2.at[slot], s2k.at[n], r2k.at[slot])

    kpair.wait_recv()
    ksend2[...] = (kgrads[...].astype(F32) + kgot1[...].astype(F32)).astype(BF16)
    for n in range(15):
        kplane(n).start()
    kgot2[spot] = ksend2[spot]

    to_after.wait_recv()
    to_before.wait_recv()

    @pl.loop(0, CAP)
    def _(t):
        spread(adj, t, pad_g, None, from_edge(north_g), from_edge(south_g))
        live = live_of(cnt, t)
        for g in range(CG):
            lanes = slice(g * 128, g * 128 + 128)
            rows = conv_tile(pad_g, taps, g, t, True)
            extra = pw[0, t] * cot[:, lanes] / TILE
            for a in range(TILE):
                g_out = live * (up[t, a, :, lanes].astype(F32) + extra)
                out[t, a, :, lanes] = (live * (g_out + rows[a])).astype(BF16)

    out_copy = pltpu.make_async_copy(out, out_hbm, out_sems.at[0])
    out_copy.start()
    down.wait_send()
    upward.wait_send()
    across.wait_recv()
    emb_both = emb_sum[0:1] + emb2[0:1]
    high = emb_both.astype(BF16).astype(F32)
    mine = jnp.where(core == 0, high, emb_both - high)
    for h in range(HID // CHUNK):
        pair_of(h).wait_send()
    emb_pair.wait_send()
    kpair.wait_send()
    to_after.wait_send()
    to_before.wait_send()

    for n in range(15):
        kplane(n, True).wait_recv()
        q, device = plane_device(*PLANE_ORDER[n])
        for hh in range(2):
            copy_to(device, send2.at[0, 0], got2.at[q, hh], s2.at[0, 0], r2.at[q, hh]).wait_recv()

    total = [got2[0, hh].astype(F32) for hh in range(2)]
    tail = kgot2[0].astype(F32)
    for q in range(1, 16):
        total = [total[hh] + got2[q, hh].astype(F32) for hh in range(2)]
        tail = tail + kgot2[q].astype(F32)

    pl.semaphore_wait(heard.at[2], 2)

    for q in range(16):
        row = q % 8 * 3
        send3[q] = jnp.concatenate([total[q // 8][row : row + 3], tail, mine], axis=0).astype(BF16)

    def ring(k, arriving=False):
        q = wrapped(z + k, 16)
        slot = q if arriving else z
        return copy_to(at(dp, plane, q), send3.at[q], got3.at[slot], s3.at[k], r3.at[slot])

    for k in RING_ORDER:
        ring(k).start()

    got3[z] = send3[z]
    across.wait_send()
    for h in range(HID // CHUNK):

        for k in DP_ORDER:
            plane_of(h, k).wait_send()

        @pl.when(plane != h // 2)
        def _():
            plane_of(h, 0).wait_send()

    for n in range(15):
        kplane(n).wait_send()
    for k in RING_ORDER:
        ring(k, True).wait_recv()

    total = got3[0].astype(F32)
    for q in range(1, 16):
        total = total + got3[q].astype(F32)

    send4[...] = total.astype(BF16)
    half[...] = jnp.broadcast_to(total[7:8], (8, C))

    def last(n, arriving=False):
        q, device = plane_device(*PLANE_ORDER[n])
        slot = q if arriving else spot
        return copy_to(device, send4, got4.at[slot], s4.at[n], r4.at[slot])

    for n in range(15):
        last(n).start()

    swap = copy_to(partner, half, other, s5.at[0], r5.at[0])
    swap.start()
    own_copy = pltpu.make_async_copy(send4, got4.at[spot], out_sems.at[1])
    own_copy.start()

    for k in RING_ORDER:
        ring(k).wait_send()

    swap.wait()
    emb_out[...] = half[...] + other[...]
    emb_copy = pltpu.make_async_copy(emb_out, emb_hbm, out_sems.at[2])
    emb_copy.start()
    out_copy.wait()
    own_copy.wait()
    emb_copy.wait()

    for n in range(15):
        last(n, True).wait_recv()
    for n in range(15):
        last(n).wait_send()


def finish_kernel(out, got4_in, emb_in, emb, tiles, w_grad, k_grad, got4, emb_got, sems):
    plane = lax.axis_index("space") // 32
    loads = [
        pltpu.make_async_copy(got4_in, got4, sems.at[0]),
        pltpu.make_async_copy(emb_in, emb_got, sems.at[1]),
        pltpu.make_async_copy(out, tiles, sems.at[2]),
    ]
    for load in loads:
        load.start()
    loads[0].wait()
    for d in range(8):
        w_grad[d * 3 : d * 3 + 3, :] = got4[d * 2 + plane, 0:3].astype(F32)
    for ij in range(49):
        row = got4[ij // 4, 3 + ij % 4 : 4 + ij % 4].astype(F32)
        k_grad[ij // 7, ij % 7 : ij % 7 + 1, :] = row
    loads[1].wait()
    emb[...] = emb_got[0:1]
    loads[2].wait()


VMEM = pl.BlockSpec(memory_space=pltpu.VMEM)
SMEM = pl.BlockSpec(memory_space=pltpu.SMEM)
HBM = pl.BlockSpec(memory_space=pltpu.HBM)


def vmem(shape, dtype):
    return pltpu.VMEM(shape, dtype)


def per_device(
    tiles_in, upstream, pool_weight, slide_cot, adjacency, counts, kernel, norm_gain, w_in, w_out,
    layer_scale,
):
    own, up = tiles_in[0], upstream[0]
    spaces = lax.axis_size("space")
    struct = jax.ShapeDtypeStruct
    dma = pltpu.SemaphoreType.DMA
    edge = (CG, CAP, 3, TILE, 128)
    halo = (CAP, 3, TILE, C)
    blocks = (CG, CAP, TILE, TILE, 128)
    chunks = HID // CHUNK

    out, got4, emb = pl.pallas_call(
        functools.partial(main_kernel, spaces),
        out_shape=(
            struct((CAP, TILE, TILE, C), BF16),
            struct((16, 8, C), BF16),
            struct((8, C), F32),
        ),
        in_specs=[SMEM] * 3 + [HBM] * 8,
        out_specs=(HBM,) * 3,
        scratch_shapes=[
            vmem((CAP, TILE, TILE, C), BF16),
            vmem((8, C), F32),
            dma((3,)),
            vmem((CAP, TILE, TILE, C), BF16),
            vmem(halo, BF16),
            vmem(halo, BF16),
            vmem((CAP, TILE, TILE, C), BF16),
            vmem((1, C), F32),
            vmem((7, 7, C), F32),
            vmem((C,), F32),
            vmem((C,), F32),
            vmem((C, HID), BF16),
            vmem((HID, C), BF16),
            dma((8,)),
            vmem((CG, CAP, 14, 24, 128), F32),
            vmem((CG, CAP, 14, 24, 128), F32),
            vmem((CG, 49, 8, 128), F32),
            vmem(blocks, F32),
            vmem((CAP, 64, 128), F32),
            vmem((PIX, C), BF16),
            vmem((PIX, C), BF16),
            vmem((PIX, C), F32),
            vmem((PIX, HID), F32),
            vmem((PIX, HID), F32),
            vmem((CHUNK, CHUNK), BF16),
            vmem(blocks, F32),
            vmem((CG, 49, 8, 128), F32),
            vmem((2, chunks, 8, 24, C), BF16),
            vmem((chunks, 8, 24, C), BF16),
            vmem((chunks, 8, 24, C), BF16),
            vmem((16, 2, 24, C), BF16),
            vmem((16, 4, C), BF16),
            vmem((16, 4, C), BF16),
            vmem((16, 4, C), BF16),
            vmem((16, 4, C), BF16),
            vmem((8, C), F32),
            vmem((8, C), F32),
            vmem((8, C), F32),
            vmem((8, C), F32),
            vmem((16, 8, C), BF16),
            vmem((16, 8, C), BF16),
            vmem((8, C), BF16),
            vmem((8, C), F32),
            vmem((8, C), F32),
            vmem(edge, BF16),
            vmem(edge, BF16),
            vmem(edge, BF16),
            vmem(edge, BF16),
            pltpu.SemaphoreType.REGULAR((3,)),
            dma((2,)), dma((2,)),
            dma((2,)), dma((2,)),
            dma((chunks,)), dma((chunks,)),
            dma((1,)), dma((1,)),
            dma((chunks, 8)), dma((16, 2)),
            dma((16,)), dma((16,)),
            dma((2,)), dma((2,)),
            dma((16,)), dma((16,)),
            dma((16,)), dma((16,)),
            dma((1,)), dma((1,)),
        ],
        compiler_params=pltpu.CompilerParams(
            collective_id=0, has_side_effects=True, vmem_limit_bytes=VMEM_BYTES
        ),
        name="main",
    )(
        pool_weight, adjacency[0], counts, own, up, slide_cot, kernel, norm_gain, layer_scale, w_in,
        w_out,
    )

    embedding, grad_tiles, w_grad, k_grad = pl.pallas_call(
        finish_kernel,
        out_shape=(
            struct((1, C), F32),
            struct((CAP, TILE, TILE, C), BF16),
            struct((24, C), F32),
            struct((7, 7, C), F32),
        ),
        in_specs=[HBM] * 3,
        out_specs=(VMEM,) * 4,
        scratch_shapes=[vmem((16, 8, C), BF16), vmem((8, C), F32), dma((3,))],
        name="finish",
    )(out, got4, emb)
    return embedding, grad_tiles[None], w_grad, k_grad


def solution(mesh):
    return jax.shard_map(
        per_device,
        mesh=mesh,
        in_specs=(
            P("dp", "space", None, None, None),
            P("dp", "space", None, None, None),
            P("dp", "space"),
            P("dp", None),
            P("dp", "space", None),
            P("dp", "space"),
            P(),
            P(),
            P(),
            P(),
            P(),
        ),
        out_specs=(P("dp", None), P("dp", "space", None, None, None), P("space", None), P()),
        check_vma=False,
    )
```
